128 devices in a mesh: ad: 32 (over z, y, core), tp: 4 (over x).
Axes of the slice: x: 4, y: 4, z: 4, core: 2. Of those that a mesh axis runs over, the one named last changes fastest.
Arguments:
- hidden: bfloat16 [1024, 8192], P('ad', 'tp'), may hold values from -6 to 6
- queries: bfloat16 [1024, 64, 128], P('ad', 'tp'), may hold values from -170 to 170
- key_cache_rows: bfloat16 [1024, 8, 128, 128], P('ad', 'tp'), may hold values from -6 to 6
- value_cache_rows: bfloat16 [1024, 8, 128, 128], P('ad', 'tp'), may hold values from -6 to 6
- cache_fill_length: int32 [1024], P('ad'), may hold values from 1 to 128, as said below
- adapter_choice_index: int32 [1024], P('ad'), may hold values from 0 to 2047, as said below
- key_value_weight: bfloat16 [8192, 2, 1024], P(None, None, 'tp'), may hold values from -0.0625 to 0.0625
- adapter_down_weight: bfloat16 [2048, 16, 8192], P('ad', None, 'tp'), may hold values from -0.0625 to 0.0625
- adapter_up_weight: bfloat16 [2048, 16, 2, 1024], P('ad', None, None, 'tp'), may hold values from -1.5 to 1.5
Outputs:
- appended_entries: bfloat16 [1024, 2, 8, 128], P('ad', None, 'tp')
- context: bfloat16 [1024, 64, 128], P('ad', 'tp')
The draws below stay inside these ranges and needn't reach their ends.
Inputs may be any that keep to these rules, and one draw needn't show every extreme that they name: `adapter_choice_index`: adapter a is held by index a // 64 of ad. Among the 32 sequences of one index of ad, at most 4 name adapters of one holder; in every draw one holder receives exactly 4 from every index of ad. `cache_fill_length`: in every block of 32 sequences one has 128.
All inputs are finite; a program needn't handle non-finite values.
Results may differ from the reference program's by a relative error of at most 0.0053.
Values may be sent and summed in bfloat16 or wider, within the bound.
No kernel may reach another device: no remote copies, remote signals or barrier semaphores. Data moves between devices by JAX's collectives and lax.ppermute only.
A program may use at most 128 MiB of HBM per device.

```python
import jax
import jax.numpy as jnp
from jax import lax

MODEL_WIDTH = 8192
HEADS = 64
KEY_VALUE_HEADS = 8
HEAD_WIDTH = 128
ADAPTER_RANK = 16
ADP_DEV = 64
SEQUENCES_LOCAL = 32
CTX = 128
CAP = 4
BATCH_SEQUENCES = 1024
ADAPTER_TOTAL = 2048


def shared_draw(key):
    lead_keys = jnp.clip(jax.random.normal(jax.random.fold_in(key, 13), (BATCH_SEQUENCES, KEY_VALUE_HEADS, HEAD_WIDTH)), -6.0, 6.0)
    return lead_keys


def draw_key_cache_rows(key, part):
    lead_keys = shared_draw(key)
    all_keys = jnp.clip(jax.random.normal(jax.random.fold_in(key, 14), (BATCH_SEQUENCES, KEY_VALUE_HEADS, CTX, HEAD_WIDTH)), -6.0, 6.0)
    all_keys = all_keys.at[:, :, 0, :].set(lead_keys)
    return all_keys.astype(jnp.bfloat16)


def draw_queries(key, part):
    values_drawn = jnp.clip(jax.random.normal(jax.random.fold_in(key, 15), (BATCH_SEQUENCES, HEADS, HEAD_WIDTH)), -6.0, 6.0)
    return values_drawn.astype(jnp.bfloat16)


def draw_cache_fill_length(key, part):
    block_count_total = BATCH_SEQUENCES // SEQUENCES_LOCAL
    length_rows = jax.random.randint(jax.random.fold_in(key, 21), (block_count_total, SEQUENCES_LOCAL), 1, CTX + 1)
    full_place = jax.random.randint(jax.random.fold_in(key, 22), (block_count_total, 1), 0, SEQUENCES_LOCAL)
    length_rows = jnp.where(jnp.arange(SEQUENCES_LOCAL)[None, :] == full_place, CTX, length_rows)
    return length_rows.reshape(BATCH_SEQUENCES).astype(jnp.int32)


def draw_adapter_choice_index(key, part):
    block_count_total = BATCH_SEQUENCES // SEQUENCES_LOCAL
    cache_slot_count = block_count_total * CAP
    random_noise = jax.random.randint(jax.random.fold_in(key, 31), (block_count_total, cache_slot_count), 0, 65536)
    holder_level = jax.random.randint(jax.random.fold_in(key, 32), (block_count_total,), 0, 4)
    complete_holder = jax.random.randint(jax.random.fold_in(key, 33), (), 0, block_count_total)
    holder_lookup = jnp.arange(cache_slot_count) // CAP
    extra_level = holder_level[holder_lookup] + 8 * (holder_lookup == complete_holder).astype(jnp.int32)
    cache_slot_score = (extra_level[None, :] * 65536 + random_noise) * 1024 + jnp.arange(cache_slot_count)[None, :]
    picked_score, chosen_slots = lax.top_k(cache_slot_score, SEQUENCES_LOCAL)
    owner_rows = chosen_slots // CAP
    shuffle_key = jax.random.randint(jax.random.fold_in(key, 34), (block_count_total, SEQUENCES_LOCAL), 0, 65536) * 1024 + jnp.arange(SEQUENCES_LOCAL)[None, :]
    shuffle_order = jnp.argsort(shuffle_key, axis=1, stable=True)
    owner_rows = jnp.take_along_axis(owner_rows, shuffle_order, axis=1)
    local_index = jax.random.randint(jax.random.fold_in(key, 35), (block_count_total, SEQUENCES_LOCAL), 0, ADP_DEV)
    return (owner_rows * ADP_DEV + local_index).reshape(BATCH_SEQUENCES).astype(jnp.int32)


def block_levels(stream_key, dims, pieces, least, top_value):
    loudness = 1.0
    for position, shards_of in pieces:
        heights = jax.random.uniform(jax.random.fold_in(jax.random.fold_in(stream_key, 6), position), (shards_of,), jnp.float32, least / len(pieces), top_value / len(pieces))
        loudness = loudness * jnp.repeat(jnp.exp(heights), dims[position] // shards_of).reshape((-1,) + (1,) * (len(dims) - 1 - position))
    return loudness


def normal_values(own_key, shape, scale, reach, pieces=(), kind=jnp.bfloat16):
    factor_of = block_levels(own_key, shape, pieces, -0.22, 0.18) if pieces else 1.0
    values = jax.random.normal(own_key, shape, jnp.float32) * scale * factor_of
    return jnp.minimum(jnp.maximum(values, -reach), reach).astype(kind)


def setup_inputs(seed: int = 0) -> dict:
    keys = jax.random.split(jax.random.key(seed), 10)
    hidden = normal_values(keys[0], (BATCH_SEQUENCES, MODEL_WIDTH), 1.0, 6.0, ((0, 32), (1, 4)))
    queries = draw_queries(jax.random.fold_in(keys[9], 71), 0)
    key_cache_rows = draw_key_cache_rows(jax.random.fold_in(keys[9], 71), 0)
    value_cache_rows = normal_values(keys[3], (BATCH_SEQUENCES, KEY_VALUE_HEADS, CTX, HEAD_WIDTH), 1.0, 6.0, ((0, 32), (1, 4)))
    cache_fill_length = draw_cache_fill_length(jax.random.fold_in(keys[9], 71), 0)
    adapter_choice_index = draw_adapter_choice_index(jax.random.fold_in(keys[9], 71), 0)
    key_value_weight = normal_values(keys[6], (MODEL_WIDTH, 2, KEY_VALUE_HEADS * HEAD_WIDTH), MODEL_WIDTH ** -0.5, 0.0625, ((2, 4),))
    adapter_down_weight = normal_values(keys[7], (ADAPTER_TOTAL, ADAPTER_RANK, MODEL_WIDTH), MODEL_WIDTH ** -0.5, 0.0625, ((0, 32), (2, 4)))
    adapter_up_weight = normal_values(keys[8], (ADAPTER_TOTAL, ADAPTER_RANK, 2, KEY_VALUE_HEADS * HEAD_WIDTH), ADAPTER_RANK ** -0.5, 1.5, ((0, 32), (3, 4)))
    return dict(hidden=hidden, queries=queries, key_cache_rows=key_cache_rows, value_cache_rows=value_cache_rows, cache_fill_length=cache_fill_length, adapter_choice_index=adapter_choice_index, key_value_weight=key_value_weight, adapter_down_weight=adapter_down_weight, adapter_up_weight=adapter_up_weight)


adapter_scale = 0.5
epsilon = 1e-05

def attend_block(packed):
    grouped_heads, keys_block, values_block, lengths_block, fresh_block = packed
    inverse_square_root = HEAD_WIDTH ** (-0.5)
    appended_keys = fresh_block[:, 0].astype(jnp.float32)
    new_values = fresh_block[:, 1].astype(jnp.float32)
    scores = jnp.einsum('bkgd,bkcd->bkgc', grouped_heads.astype(jnp.float32), keys_block.astype(jnp.float32)) * inverse_square_root
    self_score = jnp.einsum('rxlw,rxw->rxl', grouped_heads.astype(jnp.float32), appended_keys) * inverse_square_root
    in_cache = jnp.arange(CTX, dtype=jnp.int32)[None, :] < lengths_block[:, None]
    scores = jnp.where(in_cache[:, None, None, :], scores, jnp.float32(-1e+30))
    row_max = jnp.maximum(lax.optimization_barrier(jnp.max(scores, axis=3)), self_score)
    exp_terms = jnp.exp(scores - row_max[..., None])
    own_exp = jnp.exp(self_score - row_max)
    denominator = lax.optimization_barrier(jnp.sum(exp_terms, axis=3)) + own_exp
    weights = (exp_terms / denominator[..., None]).astype(jnp.bfloat16)
    own_weight = (own_exp / denominator).astype(jnp.bfloat16)
    context = jnp.einsum('bkgc,bkcd->bkgd', weights.astype(jnp.float32), values_block.astype(jnp.float32))
    context = context + own_weight.astype(jnp.float32)[..., None] * new_values[:, :, None, :]
    return context.astype(jnp.bfloat16)

def reference(hidden, queries, key_cache_rows, value_cache_rows, cache_fill_length, adapter_choice_index, key_value_weight, adapter_down_weight, adapter_up_weight):
    key_value_columns = 2 * KEY_VALUE_HEADS * HEAD_WIDTH
    widened = hidden.astype(jnp.float32)
    inverse = lax.rsqrt(lax.optimization_barrier(jnp.mean(widened * widened, axis=1, keepdims=True)) + epsilon)
    normed_input = (widened * inverse).astype(jnp.bfloat16)
    plain_projection_rows = jnp.dot(normed_input, key_value_weight.reshape(MODEL_WIDTH, key_value_columns), preferred_element_type=jnp.float32)
    block_count_total = BATCH_SEQUENCES // SEQUENCES_LOCAL

    def adapter_block(packed):
        block_rows, block_index_list = packed
        down_rows = adapter_down_weight[block_index_list].astype(jnp.float32)
        latent_state = jnp.einsum('sd,srd->sr', block_rows.astype(jnp.float32), down_rows).astype(jnp.bfloat16)
        up_rows = adapter_up_weight[block_index_list].reshape(block_index_list.shape[0], ADAPTER_RANK, key_value_columns).astype(jnp.float32)
        return adapter_scale * jnp.einsum('tb,tbl->tl', latent_state.astype(jnp.float32), up_rows)
    adapter_correction = lax.map(adapter_block, (normed_input.reshape(block_count_total, SEQUENCES_LOCAL, MODEL_WIDTH), adapter_choice_index.reshape(block_count_total, SEQUENCES_LOCAL)))
    adapter_correction = adapter_correction.reshape(BATCH_SEQUENCES, key_value_columns)
    appended_entries = (plain_projection_rows + adapter_correction).astype(jnp.bfloat16).reshape(BATCH_SEQUENCES, 2, KEY_VALUE_HEADS, HEAD_WIDTH)
    group_size = HEADS // KEY_VALUE_HEADS
    grouped_heads = queries.reshape(block_count_total, SEQUENCES_LOCAL, KEY_VALUE_HEADS, group_size, HEAD_WIDTH)
    context = lax.map(attend_block, (grouped_heads, key_cache_rows.reshape(block_count_total, SEQUENCES_LOCAL, KEY_VALUE_HEADS, CTX, HEAD_WIDTH), value_cache_rows.reshape(block_count_total, SEQUENCES_LOCAL, KEY_VALUE_HEADS, CTX, HEAD_WIDTH), cache_fill_length.reshape(block_count_total, SEQUENCES_LOCAL), appended_entries.reshape(block_count_total, SEQUENCES_LOCAL, 2, KEY_VALUE_HEADS, HEAD_WIDTH)))
    context = context.reshape(BATCH_SEQUENCES, HEADS, HEAD_WIDTH)
    return (appended_entries, context)
```

```python
import jax
import jax.numpy as jnp
from jax import lax
from jax.experimental import pallas as pl
from jax.experimental.pallas import tpu as pltpu
from jax.sharding import PartitionSpec as P

F32 = jnp.float32
BF16 = jnp.bfloat16
I32 = jnp.int32

MODEL_WIDTH = 8192
SEQ = 32
OWNERS = 32
ADAPTERS = 64
RANK = 16
SLAB = 2048
HALF = SLAB // 2
SLOT_ROWS = OWNERS * 8
KV = 2
GROUP = 8
HEAD = 128
CTX = 128
QROWS = SEQ * KV * GROUP
adapter_scale = 0.5
epsilon = 1e-05
NEG = -1e30

VMEM = pl.BlockSpec(memory_space=pltpu.VMEM)
SMEM = pl.BlockSpec(memory_space=pltpu.SMEM)
HBM = pl.BlockSpec(memory_space=pl.ANY)
NT = (((1,), (1,)), ((), ()))


def iota(shape, dim):
    return lax.broadcasted_iota(I32, shape, dim)


def ones_where(cond):
    return jnp.where(cond, 1.0, 0.0).astype(BF16)


def spread_ids(idx_ref, shape, dim):
    place = iota(shape, dim) & (SEQ - 1)
    out = jnp.zeros(shape, I32)
    for t in range(SEQ):
        out = jnp.where(place == t, idx_ref[t], out)
    return out


def call(kernel, out_shape, in_specs, scratch=(), out_specs=None, limit=48, cost=None):
    return pl.pallas_call(
        kernel,
        out_shape=out_shape,
        in_specs=in_specs,
        out_specs=out_specs if out_specs is not None else jax.tree.map(lambda _: VMEM, out_shape),
        scratch_shapes=list(scratch),
        compiler_params=pltpu.CompilerParams(vmem_limit_bytes=limit << 20),
        cost_estimate=cost,
    )


def slots_kernel(idx_ref, h_ref, out_ref):
    shape = (SEQ, 2 * SEQ)
    along = spread_ids(idx_ref, shape, 1)
    down = spread_ids(idx_ref, shape, 0)
    lane = iota(shape, 1)
    earlier = ((along >> 6) == (down >> 6)) & (iota(shape, 0) < (lane & (SEQ - 1)))
    place = jnp.sum(earlier.astype(I32), axis=0, keepdims=True)
    target = (along[0:1] >> 6) * 8 + place + 4 * (lane[0:1] >> 5)
    hot = ones_where(iota((SLOT_ROWS, 2 * SEQ), 0) == target)
    local = spread_ids(idx_ref, (2 * SEQ, 128), 0) & (ADAPTERS - 1)
    mark = ones_where(iota((2 * SEQ, 128), 1) == 2 * local + (iota((2 * SEQ, 128), 0) >> 5))
    rows = jnp.concatenate([h_ref[:, :HALF], h_ref[:, HALF:]], axis=0)
    out_ref[:, :HALF] = jnp.dot(hot, rows, preferred_element_type=F32).astype(BF16)
    out_ref[:, HALF:] = jnp.dot(hot, mark, preferred_element_type=F32).astype(BF16)


def down_kernel(r_ref, d_ref, t_ref):
    marks = r_ref[:, HALF:]
    pick = ones_where((iota((ADAPTERS, 128), 1) >> 1) == iota((ADAPTERS, 128), 0))
    chosen = lax.dot_general(pick, marks, NT, preferred_element_type=F32)
    rows = r_ref[:, :HALF]
    first = ((iota((256, SLOT_ROWS), 1) >> 2) & 1) == 0
    total = jnp.zeros((RANK, SLOT_ROWS), F32)
    for c in range(4):
        part = slice(256 * c, 256 * (c + 1))
        g0 = lax.dot_general(d_ref[part, :HALF], rows, NT, preferred_element_type=F32)
        g1 = lax.dot_general(d_ref[part, HALF:], rows, NT, preferred_element_type=F32)
        g = jnp.where(first, g0, g1).reshape(16, RANK, SLOT_ROWS)
        total += jnp.sum(g * chosen[16 * c : 16 * (c + 1)][:, None, :], axis=0)
    ahead = pltpu.roll(total, SLOT_ROWS - 4, 1)
    behind = pltpu.roll(total, 4, 1)
    t_ref[...] = total + jnp.where(first[:RANK], ahead, behind)


def mask_kernel(r_ref, m_ref):
    q = iota((128, RANK * 128), 1)
    spread = ones_where(iota((128, RANK * 128), 0) == 2 * (q >> 5) + (q & 1))
    m_ref[...] = jnp.dot(r_ref[:, HALF:], spread, preferred_element_type=F32).astype(BF16)


def up_kernel(x_ref, y_ref, m_ref, u_ref, z_ref):
    latent = (x_ref[...] + y_ref[...]).astype(BF16).astype(F32)
    turned = jnp.transpose(latent).astype(BF16)
    repeat = ones_where(((iota((RANK, 256), 1) >> 1) & (RANK - 1)) == iota((RANK, 256), 0))
    wide = jnp.dot(turned, repeat, preferred_element_type=F32).astype(BF16)
    sums = [jnp.zeros((SLOT_ROWS, HEAD), F32) for _ in range(KV)]
    for k in range(8):
        part = slice(256 * k, 256 * (k + 1))
        left = wide * m_ref[:, part]
        for c in range(KV):
            sums[c] += jnp.dot(left, u_ref[c, part, :], preferred_element_type=F32)
    for c in range(KV):
        z_ref[:, HEAD * c : HEAD * (c + 1)] = sums[c].astype(BF16)


def attend_kernel(len_ref, q_ref, k_ref, v_ref, u_ref, acc_ref, m_ref, l_ref, u2_ref, s_ref, p_ref, sem):
    copies = [
        pltpu.make_async_copy(u_ref.at[:, :, pl.ds(HEAD * c, HEAD)], u2_ref.at[c], sem.at[c])
        for c in range(KV)
    ]
    for copy in copies:
        copy.start()
    scale = HEAD**-0.5
    lane = iota((GROUP, CTX), 1)
    for b in range(SEQ):
        inside = lane < len_ref[b]
        for k in range(KV):
            row = (b * KV + k) * GROUP
            s = lax.dot_general(
                q_ref[row : row + GROUP, :], k_ref[b * KV + k], NT, preferred_element_type=F32
            )
            s_ref[row : row + GROUP, :] = jnp.where(inside, s * scale, NEG)
    for part in range(4):
        rows = slice(QROWS // 4 * part, QROWS // 4 * (part + 1))
        s = s_ref[rows, :]
        m = jnp.max(s, axis=1, keepdims=True)
        p = jnp.exp(s - m)
        m_ref[rows, :] = jnp.broadcast_to(m, p.shape)
        l_ref[rows, :] = jnp.broadcast_to(jnp.sum(p, axis=1, keepdims=True), p.shape)
        p_ref[rows, :] = p.astype(BF16)
    for pair in range(SEQ * KV):
        row = pair * GROUP
        acc_ref[row : row + GROUP, :] = jnp.dot(
            p_ref[row : row + GROUP, :], v_ref[pair], preferred_element_type=F32
        )
    for copy in copies:
        copy.wait()


def base_kernel(tp_ref, h0_ref, h1_ref, h2_ref, h3_ref, w_ref, out_ref, inv_ref, buf, sem):
    me = tp_ref[0]
    depth = 4 * SLAB
    order = (0, 1, 3, 2)
    shards = (h0_ref, h1_ref, h2_ref, h3_ref)
    copies = []
    for s in order:
        start = pl.multiple_of(((me + s) & 3) * depth, depth)
        copy = pltpu.make_async_copy(w_ref.at[pl.ds(start, depth)], buf.at[s], sem.at[s])
        copy.start()
        copies.append(copy)
    lane = iota((SEQ, 512), 1) & 3
    spread = ones_where((iota((128, 512), 1) >> 2) == iota((128, 512), 0))
    total = jnp.zeros((4 * SEQ, HEAD), F32)
    squares = jnp.zeros((SEQ, 128), F32)
    for s, copy in zip(order, copies):
        copy.wait()
        for half in range(2):
            blocks = [shards[s][:, 128 * i : 128 * (i + 1)] for i in range(8 * half, 8 * half + 8)]
            for block in blocks:
                wide = block.astype(F32)
                squares += wide * wide
            wide = jnp.dot(jnp.concatenate(blocks, axis=0), spread, preferred_element_type=F32)
            for i in range(8):
                one = wide[SEQ * i : SEQ * (i + 1)]
                left = jnp.concatenate([jnp.where(lane == n, one, 0.0) for n in range(4)], axis=0)
                start = 512 * (8 * half + i)
                total += jnp.dot(
                    left.astype(BF16), buf[s, start : start + 512, :], preferred_element_type=F32
                )
    out_ref[...] = total
    mean = jnp.sum(squares, axis=1, keepdims=True) / MODEL_WIDTH
    inv_ref[...] = jnp.broadcast_to(lax.rsqrt(mean + epsilon), (SEQ, 128))


def final_kernel(idx_ref, z_ref, base_ref, inv_ref, q_ref, acc_ref, m_ref, l_ref, kv_ref, ctx_ref):
    shape = (2 * SEQ, SEQ)
    along = spread_ids(idx_ref, shape, 1)
    down = spread_ids(idx_ref, shape, 0)
    row = iota(shape, 0)
    earlier = ((along >> 6) == (down >> 6)) & (iota(shape, 1) < (row & (SEQ - 1)))
    place = jnp.sum(earlier.astype(I32), axis=1, keepdims=True)
    target = (down[:, 0:1] >> 6) * 8 + place + 4 * (row[:, 0:1] >> 5)
    hot = ones_where(iota((2 * SEQ, SLOT_ROWS), 1) == target)
    delta = jnp.dot(hot, z_ref[...], preferred_element_type=F32)
    inverse = inv_ref[...]
    fresh = {}
    for j in range(2):
        for c in range(KV):
            plain = base_ref[SEQ * (2 * c + j) : SEQ * (2 * c + j + 1), :]
            extra = delta[SEQ * j : SEQ * (j + 1), HEAD * c : HEAD * (c + 1)]
            fresh[j, c] = ((plain + adapter_scale * extra) * inverse).astype(BF16)
            kv_ref[j, c] = fresh[j, c]
    lift_row = iota((QROWS, 2 * SEQ), 0)
    lift = ones_where(
        iota((QROWS, 2 * SEQ), 1) == ((lift_row >> 3) & 1) * SEQ + (lift_row >> 4)
    )
    new_key = jnp.dot(lift, jnp.concatenate([fresh[0, 0], fresh[0, 1]], axis=0), preferred_element_type=F32)
    new_value = jnp.dot(lift, jnp.concatenate([fresh[1, 0], fresh[1, 1]], axis=0), preferred_element_type=F32)
    own = jnp.sum(q_ref[...].astype(F32) * new_key, axis=1, keepdims=True) * (HEAD**-0.5)
    m = m_ref[...]
    top = jnp.maximum(m, own)
    keep = jnp.exp(m - top)
    own_exp = jnp.exp(own - top)
    denominator = keep * l_ref[...] + own_exp
    own_weight = (own_exp / denominator).astype(BF16).astype(F32)
    ctx_ref[...] = (acc_ref[...] * (keep / denominator) + own_weight * new_value).astype(BF16)


def on_device(
    hidden,
    queries,
    key_cache_rows,
    value_cache_rows,
    cache_fill_length,
    adapter_choice_index,
    key_value_weight,
    adapter_down_weight,
    adapter_up_weight,
):
    shape = jax.ShapeDtypeStruct
    owners = lax.axis_size("ad")
    me = lax.axis_index("tp").astype(I32).reshape(1)
    ring = lax.axis_size("tp")

    slots = call(slots_kernel, shape((SLOT_ROWS, HALF + 128), BF16), [SMEM, VMEM])(
        adapter_choice_index, hidden
    )
    arrived = lax.all_to_all(
        slots.reshape(owners, 8, HALF + 128), "ad", 0, 0, tiled=True
    ).reshape(SLOT_ROWS, HALF + 128)

    others = [
        lax.ppermute(hidden, "tp", [(i, (i - s) % ring) for i in range(ring)]) for s in (1, 2, 3)
    ]
    flat_queries = queries.reshape(QROWS, HEAD)
    partial, top, norm, up_halves = call(
        attend_kernel,
        (
            shape((QROWS, HEAD), F32),
            shape((QROWS, CTX), F32),
            shape((QROWS, CTX), F32),
            shape((KV, ADAPTERS * RANK, 2, HEAD), BF16),
        ),
        [SMEM, VMEM, VMEM, VMEM, HBM],
        scratch=[
            pltpu.VMEM((QROWS, CTX), F32),
            pltpu.VMEM((QROWS, CTX), BF16),
            pltpu.SemaphoreType.DMA((KV,)),
        ],
    )(
        cache_fill_length,
        flat_queries,
        key_cache_rows.reshape(SEQ * KV, CTX, HEAD),
        value_cache_rows.reshape(SEQ * KV, CTX, HEAD),
        adapter_up_weight.reshape(ADAPTERS * RANK, 2, KV * HEAD),
    )

    sums = call(down_kernel, shape((RANK, SLOT_ROWS), F32), [VMEM, VMEM])(
        arrived, adapter_down_weight.reshape(ADAPTERS * RANK, SLAB)
    )
    mask = call(mask_kernel, shape((SLOT_ROWS, RANK * 128), BF16), [VMEM])(arrived)
    sums = sums + lax.ppermute(sums, "tp", [(i, i ^ 1) for i in range(ring)])
    across = lax.ppermute(sums, "tp", [(i, ring - 1 - i) for i in range(ring)])
    corrections = call(up_kernel, shape((SLOT_ROWS, KV * HEAD), BF16), [VMEM] * 4)(
        sums, across, mask, up_halves.reshape(KV, RANK * 128, HEAD)
    )
    returned = lax.all_to_all(
        corrections.reshape(owners, 8, KV * HEAD), "ad", 0, 0, tiled=True
    ).reshape(SLOT_ROWS, KV * HEAD)

    weight_rows = (
        key_value_weight.reshape(MODEL_WIDTH, 2, KV, HEAD)
        .transpose(0, 2, 1, 3)
        .reshape(4 * MODEL_WIDTH, HEAD)
    )
    base, inverse = call(
        base_kernel,
        (shape((4 * SEQ, HEAD), F32), shape((SEQ, 128), F32)),
        [SMEM, VMEM, VMEM, VMEM, VMEM, HBM],
        scratch=[pltpu.VMEM((4, 4 * SLAB, HEAD), BF16), pltpu.SemaphoreType.DMA((4,))],
    )(me, hidden, *others, weight_rows)

    entries, context = call(
        final_kernel,
        (shape((2, KV, SEQ, HEAD), BF16), shape((QROWS, HEAD), BF16)),
        [SMEM] + [VMEM] * 7,
    )(adapter_choice_index, returned, base, inverse, flat_queries, partial, top, norm)
    return (
        entries.transpose(2, 0, 1, 3),
        context.reshape(SEQ, KV * GROUP, HEAD),
    )


def solution(mesh):
    placed = (
        P("ad", "tp"),
        P("ad", "tp", None),
        P("ad", "tp", None, None),
        P("ad", "tp", None, None),
        P("ad"),
        P("ad"),
        P(None, None, "tp"),
        P("ad", None, "tp"),
        P("ad", None, None, "tp"),
    )
    return jax.shard_map(
        on_device,
        mesh=mesh,
        in_specs=placed,
        out_specs=(P("ad", None, "tp", None), P("ad", "tp", None)),
        check_vma=False,
    )
```

```python
import jax
import jax.numpy as jnp
from jax import lax
from jax.experimental import pallas as pl
from jax.experimental.pallas import tpu as pltpu
from jax.sharding import PartitionSpec as P

F32 = jnp.float32
BF16 = jnp.bfloat16
I32 = jnp.int32

MODEL_WIDTH = 8192
SEQ = 32
OWNERS = 32
ADAPTERS = 64
RANK = 16
SLAB = 2048
HALF = SLAB // 2
SLOT_ROWS = OWNERS * 8
KV = 2
GROUP = 8
HEAD = 128
CTX = 128
PAIRS = 4
QROWS = SEQ * KV * GROUP
adapter_scale = 0.5
epsilon = 1e-05
NEG = -1e30

VMEM = pl.BlockSpec(memory_space=pltpu.VMEM)
SMEM = pl.BlockSpec(memory_space=pltpu.SMEM)
HBM = pl.BlockSpec(memory_space=pltpu.MemorySpace.HBM)
NT = (((1,), (1,)), ((), ()))


def iota(shape, dim):
    return lax.broadcasted_iota(I32, shape, dim)


def ones_where(cond):
    return jnp.where(cond, 1.0, 0.0).astype(BF16)


def spread_ids(idx_ref, shape, dim):
    place = iota(shape, dim) & (SEQ - 1)
    out = jnp.zeros(shape, I32)
    for t in range(SEQ):
        out = jnp.where(place == t, idx_ref[t], out)
    return out


def call(kernel, out_shape, in_specs, scratch=(), out_specs=None, limit=16, cost=None):
    return pl.pallas_call(
        kernel,
        out_shape=out_shape,
        in_specs=in_specs,
        out_specs=out_specs if out_specs is not None else jax.tree.map(lambda _: VMEM, out_shape),
        scratch_shapes=list(scratch),
        compiler_params=pltpu.CompilerParams(vmem_limit_bytes=limit << 20),
        cost_estimate=cost,
    )


def in_hbm(*arrays):
    return [pltpu.with_memory_space_constraint(a, pltpu.MemorySpace.HBM) for a in arrays]


def slots_kernel(idx_hbm, h_hbm, out_ref, idx_ref, h_ref, sem):
    rows_copy = pltpu.make_async_copy(h_hbm, h_ref, sem.at[0])
    ids_copy = pltpu.make_async_copy(idx_hbm, idx_ref, sem.at[1])
    ids_copy.start()
    rows_copy.start()
    ids_copy.wait()
    shape = (SEQ, 2 * SEQ)
    along = spread_ids(idx_ref, shape, 1)
    down = spread_ids(idx_ref, shape, 0)
    lane = iota(shape, 1)
    earlier = ((along >> 6) == (down >> 6)) & (iota(shape, 0) < (lane & (SEQ - 1)))
    place = jnp.sum(earlier.astype(I32), axis=0, keepdims=True)
    target = (along[0:1] >> 6) * 8 + place + 4 * (lane[0:1] >> 5)
    hot = ones_where(iota((SLOT_ROWS, 2 * SEQ), 0) == target)
    local = spread_ids(idx_ref, (2 * SEQ, 128), 0) & (ADAPTERS - 1)
    mark = ones_where(iota((2 * SEQ, 128), 1) == 2 * local + (iota((2 * SEQ, 128), 0) >> 5))
    out_ref[:, HALF:] = jnp.dot(hot, mark, preferred_element_type=F32).astype(BF16)
    rows_copy.wait()
    rows = jnp.concatenate([h_ref[:, :HALF], h_ref[:, HALF:]], axis=0)
    out_ref[:, :HALF] = jnp.dot(hot, rows, preferred_element_type=F32).astype(BF16)


def down_kernel(r_ref, d0_ref, d_hbm, t_ref, d_ref, sem):
    copies = [
        pltpu.make_async_copy(d_hbm.at[pl.ds(256 * (n + 1), 256)], d_ref.at[n], sem.at[n])
        for n in range(3)
    ]
    for copy in copies:
        copy.start()
    marks = r_ref[:, HALF:]
    pick = ones_where((iota((ADAPTERS, 128), 1) >> 1) == iota((ADAPTERS, 128), 0))
    chosen = lax.dot_general(pick, marks, NT, preferred_element_type=F32)
    rows = r_ref[:, :HALF]
    first = ((iota((256, SLOT_ROWS), 1) >> 2) & 1) == 0
    total = jnp.zeros((RANK, SLOT_ROWS), F32)
    for c in range(4):
        part = d0_ref
        if c:
            copies[c - 1].wait()
            part = d_ref.at[c - 1]
        g0 = lax.dot_general(part[:, :HALF], rows, NT, preferred_element_type=F32)
        g1 = lax.dot_general(part[:, HALF:], rows, NT, preferred_element_type=F32)
        g = jnp.where(first, g0, g1).reshape(16, RANK, SLOT_ROWS)
        total += jnp.sum(g * chosen[16 * c : 16 * (c + 1)][:, None, :], axis=0)
    ahead = pltpu.roll(total, SLOT_ROWS - 4, 1)
    behind = pltpu.roll(total, 4, 1)
    t_ref[...] = total + jnp.where(first[:RANK], ahead, behind)


def mask_kernel(r_ref, m_ref):
    q = iota((128, RANK * 128), 1)
    spread = ones_where(iota((128, RANK * 128), 0) == 2 * (q >> 5) + (q & 1))
    m_ref[...] = jnp.dot(r_ref[:, HALF:], spread, preferred_element_type=F32).astype(BF16)


def up_kernel(a_ref, b_ref, c_ref, d_ref, m_ref, u_ref, z_ref):
    latent = ((a_ref[...] + b_ref[...]) + (c_ref[...] + d_ref[...])).astype(BF16).astype(F32)
    turned = jnp.transpose(latent).astype(BF16)
    repeat = ones_where(((iota((RANK, 256), 1) >> 1) & (RANK - 1)) == iota((RANK, 256), 0))
    wide = jnp.dot(turned, repeat, preferred_element_type=F32).astype(BF16)
    sums = [jnp.zeros((SLOT_ROWS, HEAD), F32) for _ in range(KV)]
    for k in range(8):
        part = slice(256 * k, 256 * (k + 1))
        left = wide * m_ref[:, part]
        for c in range(KV):
            sums[c] += jnp.dot(left, u_ref[c, part, :], preferred_element_type=F32)
    for c in range(KV):
        z_ref[:, HEAD * c : HEAD * (c + 1)] = sums[c].astype(BF16)


def attend_kernel(
    len_hbm, q_hbm, k_hbm, v_hbm, u_ref, d_ref,
    mid_ref, lse_ref, u2_ref, d0_ref,
    len_ref, q_ref, k_ref, v_ref, s_ref, sem, in_sem,
):
    inputs = [
        pltpu.make_async_copy(source, target, in_sem.at[n])
        for n, (source, target) in enumerate(
            ((len_hbm, len_ref), (q_hbm, q_ref), (k_hbm, k_ref), (v_hbm, v_ref))
        )
    ]
    for copy in inputs:
        copy.start()
    copies = [
        pltpu.make_async_copy(u_ref.at[:, :, pl.ds(HEAD * c, HEAD)], u2_ref.at[c], sem.at[c])
        for c in range(KV)
    ]
    copies.append(pltpu.make_async_copy(d_ref.at[pl.ds(0, 256)], d0_ref, sem.at[KV]))
    for copy in copies:
        copy.start()
    scale = HEAD**-0.5
    lane = iota((GROUP, CTX), 1)
    for copy in inputs[:3]:
        copy.wait()
    for g in range(SEQ * KV // PAIRS):
        rows = slice(GROUP * PAIRS * g, GROUP * PAIRS * (g + 1))
        keys = k_ref[PAIRS * g : PAIRS * (g + 1)].reshape(PAIRS * CTX, HEAD)
        s = lax.dot_general(q_ref[rows, :], keys, NT, preferred_element_type=F32) * scale
        for n in range(PAIRS):
            pair = PAIRS * g + n
            own = s[GROUP * n : GROUP * (n + 1), CTX * n : CTX * (n + 1)]
            s_ref[GROUP * pair : GROUP * (pair + 1), :] = jnp.where(
                lane < len_ref[pair // KV], own, NEG
            )
    for part in range(4):
        rows = slice(QROWS // 4 * part, QROWS // 4 * (part + 1))
        s = s_ref[rows, :]
        m = jnp.max(s, axis=1, keepdims=True)
        p = jnp.exp(s - m)
        norm = jnp.broadcast_to(jnp.sum(p, axis=1, keepdims=True), p.shape)
        lse_ref[rows, :] = m + jnp.log(norm)
        s_ref[rows, :] = p / norm
    inputs[3].wait()
    for g in range(SEQ * KV // PAIRS):
        blocks = []
        for n in range(PAIRS):
            pair = PAIRS * g + n
            p = s_ref[GROUP * pair : GROUP * (pair + 1), :]
            zero = jnp.zeros_like(p)
            blocks.append(
                jnp.concatenate([p if k == n else zero for k in range(PAIRS)], axis=1)
            )
        values = v_ref[PAIRS * g : PAIRS * (g + 1)].reshape(PAIRS * CTX, HEAD)
        mid_ref[GROUP * PAIRS * g : GROUP * PAIRS * (g + 1), :] = jnp.dot(
            jnp.concatenate(blocks, axis=0).astype(BF16), values, preferred_element_type=F32
        )
    for copy in copies:
        copy.wait()


def inverse_rms(shards):
    squares = jnp.zeros((SEQ, 128), F32)
    for shard in shards:
        for i in range(SLAB // 128):
            wide = shard[:, 128 * i : 128 * (i + 1)].astype(F32)
            squares += wide * wide
    mean = jnp.sum(squares, axis=1, keepdims=True) / MODEL_WIDTH
    return jnp.broadcast_to(lax.rsqrt(mean + epsilon), (SEQ, 128))


def base_half(steps, tp_ref, shards, inverse, w_ref, buf, left_ref, sem):
    me = tp_ref[0]
    depth = 4 * SLAB
    copies = []
    for n, s in enumerate(steps):
        start = pl.multiple_of(((me + s) & 3) * depth, depth)
        copies.append(pltpu.make_async_copy(w_ref.at[pl.ds(start, depth)], buf.at[n], sem.at[n]))
        copies[n].start()
    inverse = inverse()
    place = iota((SEQ, 512), 1) & 3
    spread = ones_where((iota((128, 512), 1) >> 2) == iota((128, 512), 0))
    total = jnp.zeros((4 * SEQ, HEAD), F32)
    for n, shard in enumerate(shards):
        blocks = [
            (shard[:, 128 * i : 128 * (i + 1)].astype(F32) * inverse).astype(BF16)
            for i in range(SLAB // 128)
        ]
        wide = jnp.dot(jnp.concatenate(blocks, axis=0), spread, preferred_element_type=F32)
        for i in range(SLAB // 128):
            one = wide[SEQ * i : SEQ * (i + 1)]
            for k in range(4):
                left_ref[SEQ * k : SEQ * (k + 1), 512 * i : 512 * (i + 1)] = jnp.where(
                    place == k, one, 0.0
                ).astype(BF16)
        copies[n].wait()
        total += jnp.dot(left_ref[...], buf[n], preferred_element_type=F32)
    return total


def base_first_kernel(tp_ref, h0_ref, h1_ref, h2_ref, h3_ref, w_ref, out_ref, inv_ref, *scratch):
    def inverse():
        inv_ref[...] = inverse_rms((h0_ref, h1_ref, h2_ref, h3_ref))
        return inv_ref[...]

    out_ref[...] = base_half((0, 1), tp_ref, (h0_ref, h1_ref), inverse, w_ref, *scratch)


def base_last_kernel(tp_ref, h2_ref, h3_ref, inv_ref, before_ref, w_ref, out_ref, *scratch):
    out_ref[...] = before_ref[...] + base_half(
        (2, 3), tp_ref, (h2_ref, h3_ref), lambda: inv_ref[...], w_ref, *scratch
    )


def final_kernel(idx_ref, z_ref, base_ref, inv_ref, q_ref, mid_ref, lse_ref, kv_ref, ctx_ref):
    shape = (2 * SEQ, SEQ)
    along = spread_ids(idx_ref, shape, 1)
    down = spread_ids(idx_ref, shape, 0)
    row = iota(shape, 0)
    earlier = ((along >> 6) == (down >> 6)) & (iota(shape, 1) < (row & (SEQ - 1)))
    place = jnp.sum(earlier.astype(I32), axis=1, keepdims=True)
    target = (down[:, 0:1] >> 6) * 8 + place + 4 * (row[:, 0:1] >> 5)
    hot = ones_where(iota((2 * SEQ, SLOT_ROWS), 1) == target)
    delta = jnp.dot(hot, z_ref[...], preferred_element_type=F32)
    inverse = inv_ref[...]
    fresh = {}
    for j in range(2):
        for c in range(KV):
            plain = base_ref[SEQ * (2 * c + j) : SEQ * (2 * c + j + 1), :]
            extra = delta[SEQ * j : SEQ * (j + 1), HEAD * c : HEAD * (c + 1)]
            fresh[j, c] = (plain + adapter_scale * inverse * extra).astype(BF16)
            kv_ref[:, j, c, :] = fresh[j, c]
    lift_row = iota((QROWS, 2 * SEQ), 0)
    lift = ones_where(
        iota((QROWS, 2 * SEQ), 1) == ((lift_row >> 3) & 1) * SEQ + (lift_row >> 4)
    )
    new_key = jnp.dot(lift, jnp.concatenate([fresh[0, 0], fresh[0, 1]], axis=0), preferred_element_type=F32)
    new_value = jnp.dot(lift, jnp.concatenate([fresh[1, 0], fresh[1, 1]], axis=0), preferred_element_type=F32)
    own = jnp.sum(q_ref[...].astype(F32) * new_key, axis=1, keepdims=True) * (HEAD**-0.5)
    gap = own - lse_ref[...]
    small = jnp.exp(-jnp.abs(gap))
    share = jnp.where(gap > 0, 1.0, small) / (1.0 + small)
    own_weight = share.astype(BF16).astype(F32)
    ctx_ref[...] = (mid_ref[...] * (1.0 - share) + own_weight * new_value).astype(BF16)


def on_device(
    hidden,
    queries,
    key_cache_rows,
    value_cache_rows,
    cache_fill_length,
    adapter_choice_index,
    key_value_weight,
    adapter_down_weight,
    adapter_up_weight,
):
    shape = jax.ShapeDtypeStruct
    owners = lax.axis_size("ad")
    ring = lax.axis_size("tp")

    slots = call(
        slots_kernel,
        shape((SLOT_ROWS, HALF + 128), BF16),
        [HBM, HBM],
        scratch=[
            pltpu.SMEM((SEQ,), I32),
            pltpu.VMEM((SEQ, SLAB), BF16),
            pltpu.SemaphoreType.DMA((2,)),
        ],
    )(*in_hbm(adapter_choice_index, hidden))
    slots, rows_here, fill = lax.optimization_barrier((slots, hidden, cache_fill_length))
    arrived = lax.all_to_all(
        slots.reshape(owners, 8, HALF + 128), "ad", 0, 0, tiled=True
    ).reshape(SLOT_ROWS, HALF + 128)

    others = [
        lax.ppermute(rows_here, "tp", [(i, (i - s) % ring) for i in range(ring)]) for s in (1, 2, 3)
    ]
    flat_queries = queries.reshape(QROWS, HEAD)
    middle, level, up_halves, down = call(
        attend_kernel,
        (
            shape((QROWS, HEAD), F32),
            shape((QROWS, CTX), F32),
            pltpu.VMEM((KV, ADAPTERS * RANK, 2, HEAD), BF16),
            pltpu.VMEM((256, SLAB), BF16),
        ),
        [HBM] * 6,
        scratch=[
            pltpu.SMEM((SEQ,), I32),
            pltpu.VMEM((QROWS, HEAD), BF16),
            pltpu.VMEM((SEQ * KV, CTX, HEAD), BF16),
            pltpu.VMEM((SEQ * KV, CTX, HEAD), BF16),
            pltpu.VMEM((QROWS, CTX), F32),
            pltpu.SemaphoreType.DMA((KV + 1,)),
            pltpu.SemaphoreType.DMA((4,)),
        ],
        cost=pl.CostEstimate(flops=1 << 30, transcendentals=1 << 16, bytes_accessed=12 << 20),
    )(
        *in_hbm(
            fill,
            flat_queries,
            key_cache_rows.reshape(SEQ * KV, CTX, HEAD),
            value_cache_rows.reshape(SEQ * KV, CTX, HEAD),
            adapter_up_weight.reshape(ADAPTERS * RANK, 2, KV * HEAD),
            adapter_down_weight.reshape(ADAPTERS * RANK, SLAB),
        )
    )
    arrived, middle, rows_here = lax.optimization_barrier((arrived, middle, rows_here))
    sums = call(
        down_kernel,
        shape((RANK, SLOT_ROWS), F32),
        [VMEM, VMEM, HBM],
        scratch=[pltpu.VMEM((3, 256, SLAB), BF16), pltpu.SemaphoreType.DMA((3,))],
    )(arrived, down, *in_hbm(adapter_down_weight.reshape(ADAPTERS * RANK, SLAB)))
    mask = call(mask_kernel, shape((SLOT_ROWS, RANK * 128), BF16), [VMEM])(arrived)
    shares = [
        lax.ppermute(sums, "tp", [(i, (i + s) % ring) for i in range(ring)]) for s in (1, 3, 2)
    ]
    me = lax.axis_index("tp").astype(I32).reshape(1)
    weight_rows = (
        key_value_weight.reshape(MODEL_WIDTH, 2, KV, HEAD)
        .transpose(0, 2, 1, 3)
        .reshape(4 * MODEL_WIDTH, HEAD)
    )
    half_scratch = [
        pltpu.VMEM((2, 4 * SLAB, HEAD), BF16),
        pltpu.VMEM((4 * SEQ, 4 * SLAB), BF16),
        pltpu.SemaphoreType.DMA((2,)),
    ]
    base, inverse = call(
        base_first_kernel,
        (shape((4 * SEQ, HEAD), F32), shape((SEQ, 128), F32)),
        [SMEM, VMEM, VMEM, VMEM, VMEM, HBM],
        scratch=half_scratch,
    )(me, hidden, *others, *in_hbm(weight_rows))
    shares, base = lax.optimization_barrier((shares, base))
    corrections = call(up_kernel, shape((SLOT_ROWS, KV * HEAD), BF16), [VMEM] * 6)(
        sums, *shares, mask, up_halves.reshape(KV, RANK * 128, HEAD)
    )
    returned = lax.all_to_all(
        corrections.reshape(owners, 8, KV * HEAD), "ad", 0, 0, tiled=True
    ).reshape(SLOT_ROWS, KV * HEAD)

    base = call(
        base_last_kernel,
        shape((4 * SEQ, HEAD), F32),
        [SMEM, VMEM, VMEM, VMEM, VMEM, HBM],
        scratch=half_scratch,
    )(me, *others[1:], inverse, base, *in_hbm(weight_rows))

    entries, context = call(
        final_kernel,
        (shape((SEQ, 2, KV, HEAD), BF16), shape((QROWS, HEAD), BF16)),
        [SMEM] + [VMEM] * 6,
    )(adapter_choice_index, returned, base, inverse, flat_queries, middle, level)
    return (
        entries,
        context.reshape(SEQ, KV * GROUP, HEAD),
    )


def solution(mesh):
    placed = (
        P("ad", "tp"),
        P("ad", "tp", None),
        P("ad", "tp", None, None),
        P("ad", "tp", None, None),
        P("ad"),
        P("ad"),
        P(None, None, "tp"),
        P("ad", None, "tp"),
        P("ad", None, None, "tp"),
    )
    return jax.shard_map(
        on_device,
        mesh=mesh,
        in_specs=placed,
        out_specs=(P("ad", None, "tp", None), P("ad", "tp", None)),
        check_vma=False,
    )
```

```python
import jax
import jax.numpy as jnp
from jax import lax
from jax.experimental import pallas as pl
from jax.experimental.pallas import tpu as pltpu
from jax.sharding import PartitionSpec as P

F32 = jnp.float32
BF16 = jnp.bfloat16
I32 = jnp.int32

MODEL_WIDTH = 8192
SEQ = 32
OWNERS = 32
ADAPTERS = 64
RANK = 16
HELD_PARTS = ((0, 256), (256, 256))
HELD = 512
PIECES = ((512, 256), (768, 256))
SLAB = 2048
HALF = SLAB // 2
DEPTH = 4 * SLAB
SLOT_ROWS = OWNERS * 8
KV = 2
GROUP = 8
HEAD = 128
CTX = 128
PAIRS = 4
QROWS = SEQ * KV * GROUP
adapter_scale = 0.5
epsilon = 1e-05
NEG = -1e30

VMEM = pl.BlockSpec(memory_space=pltpu.VMEM)
SMEM = pl.BlockSpec(memory_space=pltpu.SMEM)
HBM = pl.BlockSpec(memory_space=pltpu.MemorySpace.HBM)
NT = (((1,), (1,)), ((), ()))


def iota(shape, dim):
    return lax.broadcasted_iota(I32, shape, dim)


def ones_where(cond):
    return jnp.where(cond, 1.0, 0.0).astype(BF16)


def spread_ids(idx_ref, shape, dim):
    place = iota(shape, dim) & (SEQ - 1)
    out = jnp.zeros(shape, I32)
    for t in range(SEQ):
        out = jnp.where(place == t, idx_ref[t], out)
    return out


def call(kernel, out_shape, in_specs, scratch=(), out_specs=None, limit=16, cost=None):
    return pl.pallas_call(
        kernel,
        out_shape=out_shape,
        in_specs=in_specs,
        out_specs=out_specs if out_specs is not None else jax.tree.map(lambda _: VMEM, out_shape),
        scratch_shapes=list(scratch),
        compiler_params=pltpu.CompilerParams(vmem_limit_bytes=limit << 20),
        cost_estimate=cost,
    )


def in_hbm(*arrays):
    return [pltpu.with_memory_space_constraint(a, pltpu.MemorySpace.HBM) for a in arrays]


def slots_kernel(idx_hbm, h_hbm, out_hbm, idx_ref, h_ref, out_ref, sem, out_sem):
    rows_copy = pltpu.make_async_copy(h_hbm, h_ref, sem.at[0])
    ids_copy = pltpu.make_async_copy(idx_hbm, idx_ref, sem.at[1])
    ids_copy.start()
    rows_copy.start()
    ids_copy.wait()
    shape = (SEQ, 2 * SEQ)
    along = spread_ids(idx_ref, shape, 1)
    down = spread_ids(idx_ref, shape, 0)
    lane = iota(shape, 1)
    earlier = ((along >> 6) == (down >> 6)) & (iota(shape, 0) < (lane & (SEQ - 1)))
    place = jnp.sum(earlier.astype(I32), axis=0, keepdims=True)
    target = (along[0:1] >> 6) * 8 + place + 4 * (lane[0:1] >> 5)
    hot = ones_where(iota((SLOT_ROWS, 2 * SEQ), 0) == target)
    local = spread_ids(idx_ref, (2 * SEQ, 128), 0) & (ADAPTERS - 1)
    mark = ones_where(iota((2 * SEQ, 128), 1) == 2 * local + (iota((2 * SEQ, 128), 0) >> 5))
    out_ref[:, HALF:] = jnp.dot(hot, mark, preferred_element_type=F32).astype(BF16)
    rows_copy.wait()
    rows = jnp.concatenate([h_ref[:, :HALF], h_ref[:, HALF:]], axis=0)
    copies = []
    for n in range(4):
        part = slice(SLOT_ROWS // 4 * n, SLOT_ROWS // 4 * (n + 1))
        out_ref[part, :HALF] = jnp.dot(hot[part], rows, preferred_element_type=F32).astype(BF16)
        copies.append(pltpu.make_async_copy(out_ref.at[part], out_hbm.at[part], out_sem.at[n]))
        copies[n].start()
    for copy in copies:
        copy.wait()


def down_kernel(r_ref, held_ref, d_hbm, t_ref, d_ref, sem):
    copies = []
    for n, (start, count) in enumerate(PIECES):
        rows = pl.ds(start - HELD, count)
        copies.append(
            pltpu.make_async_copy(d_hbm.at[pl.ds(start, count)], d_ref.at[rows], sem.at[n])
        )
        copies[n].start()
    marks = r_ref[:, HALF:]
    pick = ones_where((iota((ADAPTERS, 128), 1) >> 1) == iota((ADAPTERS, 128), 0))
    chosen = lax.dot_general(pick, marks, NT, preferred_element_type=F32)
    rows = r_ref[:, :HALF]

    def product(part, start, count):
        first = ((iota((count, SLOT_ROWS), 1) >> 2) & 1) == 0
        g0 = lax.dot_general(part[:, :HALF], rows, NT, preferred_element_type=F32)
        g1 = lax.dot_general(part[:, HALF:], rows, NT, preferred_element_type=F32)
        g = jnp.where(first, g0, g1).reshape(count // RANK, RANK, SLOT_ROWS)
        mine = chosen[start // RANK : (start + count) // RANK]
        return jnp.sum(g * mine[:, None, :], axis=0)

    total = jnp.zeros((RANK, SLOT_ROWS), F32)
    for start, count in HELD_PARTS:
        total += product(held_ref.at[pl.ds(start, count)], start, count)
    for n, (start, count) in enumerate(PIECES):
        copies[n].wait()
        total += product(d_ref.at[pl.ds(start - HELD, count)], start, count)
    first = ((iota((RANK, SLOT_ROWS), 1) >> 2) & 1) == 0
    ahead = pltpu.roll(total, SLOT_ROWS - 4, 1)
    behind = pltpu.roll(total, 4, 1)
    t_ref[...] = total + jnp.where(first, ahead, behind)


def up_kernel(a_ref, b_ref, m_ref, u_ref, z_ref):
    latent = (a_ref[...] + b_ref[...]).astype(BF16).astype(F32)
    turned = jnp.transpose(latent).astype(BF16)
    repeat = ones_where(((iota((RANK, 256), 1) >> 1) & (RANK - 1)) == iota((RANK, 256), 0))
    wide = jnp.dot(turned, repeat, preferred_element_type=F32).astype(BF16)
    total = jnp.zeros((SLOT_ROWS, KV * HEAD), F32)
    for k in range(8):
        part = slice(256 * k, 256 * (k + 1))
        right = jnp.concatenate([u_ref[c, part, :] for c in range(KV)], axis=1)
        total += jnp.dot(wide * m_ref[:, part], right, preferred_element_type=F32)
    z_ref[...] = total.astype(BF16)


def returned_rows(idx_ref, hot_ref):
    shape = (2 * SEQ, SEQ)
    along = spread_ids(idx_ref, shape, 1)
    down = spread_ids(idx_ref, shape, 0)
    row = iota(shape, 0)
    earlier = ((along >> 6) == (down >> 6)) & (iota(shape, 1) < (row & (SEQ - 1)))
    place = jnp.sum(earlier.astype(I32), axis=1, keepdims=True)
    target = (down[:, 0:1] >> 6) * 8 + place + 4 * (row[:, 0:1] >> 5)
    hot_ref[...] = ones_where(iota((2 * SEQ, SLOT_ROWS), 1) == target)
def query_tokens(lift_ref):
    lift_row = iota((QROWS, 2 * SEQ), 0)
    lift_ref[...] = ones_where(
        iota((QROWS, 2 * SEQ), 1) == ((lift_row >> 3) & 1) * SEQ + (lift_row >> 4)
    )


def inverse_rms(shards):
    squares = jnp.zeros((SEQ, 128), F32)
    for shard in shards:
        for i in range(SLAB // 128):
            wide = shard[:, 128 * i : 128 * (i + 1)].astype(F32)
            squares += wide * wide
    mean = jnp.sum(squares, axis=1, keepdims=True) / MODEL_WIDTH
    return jnp.broadcast_to(lax.rsqrt(mean + epsilon), (SEQ, 128))


def start_weights(tp_ref, steps, w_ref, buf, sem):
    me = tp_ref[0]
    copies = []
    for n, s in enumerate(steps):
        for k in range(2):
            start = pl.multiple_of(((me + s) & 3) * DEPTH + k * (DEPTH // 2), DEPTH // 2)
            place = 2 * n + k
            copies.append(
                pltpu.make_async_copy(
                    w_ref.at[pl.ds(start, DEPTH // 2)], buf.at[place], sem.at[place]
                )
            )
            copies[place].start()
    return copies


def base_part(shards, inverse, copies, buf, left_ref):
    place = iota((SEQ, 512), 1) & 3
    spread = ones_where((iota((128, 512), 1) >> 2) == iota((128, 512), 0))
    total = jnp.zeros((4 * SEQ, HEAD), F32)
    for n, shard in enumerate(shards):
        blocks = [shard[:, 128 * i : 128 * (i + 1)] for i in range(SLAB // 128)]
        if inverse is not None:
            blocks = [(block.astype(F32) * inverse).astype(BF16) for block in blocks]
        wide = jnp.dot(jnp.concatenate(blocks, axis=0), spread, preferred_element_type=F32)
        for i in range(SLAB // 128):
            one = wide[SEQ * i : SEQ * (i + 1)]
            for k in range(4):
                left_ref[SEQ * k : SEQ * (k + 1), 512 * i : 512 * (i + 1)] = jnp.where(
                    place == k, one, 0.0
                ).astype(BF16)
        for k in range(2):
            copies[2 * n + k].wait()
            total += jnp.dot(
                left_ref[:, DEPTH // 2 * k : DEPTH // 2 * (k + 1)],
                buf[2 * n + k],
                preferred_element_type=F32,
            )
    return total


def attend_kernel(
    tp_ref, len_hbm, idx_hbm, q_hbm, k_hbm, v_hbm, h_hbm, d_ref, w_ref,
    mid_hbm, lse_hbm, hot_ref, d0_ref, base_ref,
    len_ref, idx_ref, q_ref, k_ref, v_ref, h_ref, s_ref, mid_ref, lse_ref, buf, left_ref,
    sem, in_sem, w_sem,
):
    inputs = [
        pltpu.make_async_copy(source, target, in_sem.at[n])
        for n, (source, target) in enumerate(
            ((len_hbm, len_ref), (idx_hbm, idx_ref), (q_hbm, q_ref), (k_hbm, k_ref), (v_hbm, v_ref), (h_hbm, h_ref))
        )
    ]
    for copy in inputs:
        copy.start()
    down_copy = pltpu.make_async_copy(d_ref.at[pl.ds(0, HELD)], d0_ref, sem.at[0])
    weights = start_weights(tp_ref, (0,), w_ref, buf, w_sem)
    down_copy.start()
    inputs[0].wait()
    inputs[1].wait()
    returned_rows(idx_ref, hot_ref)
    scale = HEAD**-0.5
    lane = iota((GROUP, CTX), 1)
    inputs[2].wait()
    inputs[3].wait()
    for g in range(SEQ * KV // PAIRS):
        rows = slice(GROUP * PAIRS * g, GROUP * PAIRS * (g + 1))
        keys = k_ref[PAIRS * g : PAIRS * (g + 1)].reshape(PAIRS * CTX, HEAD)
        s = lax.dot_general(q_ref[rows, :], keys, NT, preferred_element_type=F32) * scale
        for n in range(PAIRS):
            pair = PAIRS * g + n
            own = s[GROUP * n : GROUP * (n + 1), CTX * n : CTX * (n + 1)]
            s_ref[GROUP * pair : GROUP * (pair + 1), :] = jnp.where(
                lane < len_ref[pair // KV], own, NEG
            )
    for part in range(4):
        rows = slice(QROWS // 4 * part, QROWS // 4 * (part + 1))
        s = s_ref[rows, :]
        m = jnp.max(s, axis=1, keepdims=True)
        p = jnp.exp(s - m)
        norm = jnp.broadcast_to(jnp.sum(p, axis=1, keepdims=True), p.shape)
        lse_ref[rows, :] = m + jnp.log(norm)
        s_ref[rows, :] = p / norm
    level_copy = pltpu.make_async_copy(lse_ref, lse_hbm, sem.at[1])
    level_copy.start()
    inputs[4].wait()
    for g in range(SEQ * KV // PAIRS):
        blocks = []
        for n in range(PAIRS):
            pair = PAIRS * g + n
            p = s_ref[GROUP * pair : GROUP * (pair + 1), :]
            zero = jnp.zeros_like(p)
            blocks.append(
                jnp.concatenate([p if k == n else zero for k in range(PAIRS)], axis=1)
            )
        values = v_ref[PAIRS * g : PAIRS * (g + 1)].reshape(PAIRS * CTX, HEAD)
        mid_ref[GROUP * PAIRS * g : GROUP * PAIRS * (g + 1), :] = jnp.dot(
            jnp.concatenate(blocks, axis=0).astype(BF16), values, preferred_element_type=F32
        )
    middle_copy = pltpu.make_async_copy(mid_ref, mid_hbm, sem.at[2])
    middle_copy.start()
    inputs[5].wait()
    base_ref[...] = base_part((h_ref,), None, weights, buf, left_ref)
    for copy in (down_copy, level_copy, middle_copy):
        copy.wait()


def between_kernel(
    tp_ref, r_ref, h0_ref, h1_ref, h2_ref, h3_ref, before_ref, u_ref, w_ref,
    mask_ref, inv_ref, u2_ref, out_ref, buf, left_ref, w_sem, sem,
):
    copies = [
        pltpu.make_async_copy(u_ref.at[:, :, pl.ds(HEAD * c, HEAD)], u2_ref.at[c], sem.at[c])
        for c in range(KV)
    ]
    for copy in copies:
        copy.start()
    weights = start_weights(tp_ref, (1,), w_ref, buf, w_sem)
    q = iota((128, RANK * 128), 1)
    spread = ones_where(iota((128, RANK * 128), 0) == 2 * (q >> 5) + (q & 1))
    mask_ref[...] = jnp.dot(r_ref[:, HALF:], spread, preferred_element_type=F32).astype(BF16)
    inverse = inverse_rms((h0_ref, h1_ref, h2_ref, h3_ref))
    inv_ref[...] = inverse
    total = base_part((h1_ref,), inverse, weights, buf, left_ref)
    for k in range(4):
        rows = slice(SEQ * k, SEQ * (k + 1))
        out_ref[rows, :] = total[rows] + before_ref[rows, :] * inverse
    for copy in copies:
        copy.wait()


def base_kernel(
    tp_ref, h2_ref, h3_ref, inv_ref, before_ref, w_ref,
    out_ref, lift_ref, buf, left_ref, sem,
):
    copies = start_weights(tp_ref, (2, 3), w_ref, buf, sem)
    query_tokens(lift_ref)
    out_ref[...] = before_ref[...] + base_part(
        (h2_ref, h3_ref), inv_ref[...], copies, buf, left_ref
    )


def final_kernel(hot_ref, lift_ref, z_ref, base_ref, inv_ref, q_ref, mid_ref, lse_ref, kv_ref, ctx_ref):
    lift = lift_ref[...]
    delta = jnp.dot(hot_ref[...], z_ref[...], preferred_element_type=F32)
    inverse = inv_ref[...]
    fresh = {}
    for j in range(2):
        for c in range(KV):
            plain = base_ref[SEQ * (2 * c + j) : SEQ * (2 * c + j + 1), :]
            extra = delta[SEQ * j : SEQ * (j + 1), HEAD * c : HEAD * (c + 1)]
            fresh[j, c] = (plain + adapter_scale * inverse * extra).astype(BF16)
            kv_ref[:, j, c, :] = fresh[j, c]
    new_key = jnp.dot(lift, jnp.concatenate([fresh[0, 0], fresh[0, 1]], axis=0), preferred_element_type=F32)
    new_value = jnp.dot(lift, jnp.concatenate([fresh[1, 0], fresh[1, 1]], axis=0), preferred_element_type=F32)
    own = jnp.sum(q_ref[...].astype(F32) * new_key, axis=1, keepdims=True) * (HEAD**-0.5)
    gap = own - lse_ref[...]
    small = jnp.exp(-jnp.abs(gap))
    share = jnp.where(gap > 0, 1.0, small) / (1.0 + small)
    own_weight = share.astype(BF16).astype(F32)
    ctx_ref[...] = (mid_ref[...] * (1.0 - share) + own_weight * new_value).astype(BF16)


def on_device(
    hidden,
    queries,
    key_cache_rows,
    value_cache_rows,
    cache_fill_length,
    adapter_choice_index,
    key_value_weight,
    adapter_down_weight,
    adapter_up_weight,
):
    shape = jax.ShapeDtypeStruct
    owners = lax.axis_size("ad")
    ring = lax.axis_size("tp")

    slots = call(
        slots_kernel,
        shape((SLOT_ROWS, HALF + 128), BF16),
        [HBM, HBM],
        out_specs=HBM,
        scratch=[
            pltpu.SMEM((SEQ,), I32),
            pltpu.VMEM((SEQ, SLAB), BF16),
            pltpu.VMEM((SLOT_ROWS, HALF + 128), BF16),
            pltpu.SemaphoreType.DMA((2,)),
            pltpu.SemaphoreType.DMA((4,)),
        ],
    )(*in_hbm(adapter_choice_index, hidden))
    slots, rows_here, fill = lax.optimization_barrier((slots, hidden, cache_fill_length))
    arrived = lax.all_to_all(
        slots.reshape(owners, 8, HALF + 128), "ad", 0, 0, tiled=True
    ).reshape(SLOT_ROWS, HALF + 128)

    others = [
        lax.ppermute(rows_here, "tp", [(i, (i - s) % ring) for i in range(ring)]) for s in (1, 2, 3)
    ]
    flat_queries = queries.reshape(QROWS, HEAD)
    me = lax.axis_index("tp").astype(I32).reshape(1)
    weight_rows = (
        key_value_weight.reshape(MODEL_WIDTH, 2, KV, HEAD)
        .transpose(0, 2, 1, 3)
        .reshape(4 * MODEL_WIDTH, HEAD)
    )

    def weight_scratch(count):
        return [
            pltpu.VMEM((2 * count, DEPTH // 2, HEAD), BF16),
            pltpu.VMEM((4 * SEQ, DEPTH), BF16),
        ]

    middle, level, hot, down, base = call(
        attend_kernel,
        (
            pltpu.MemorySpace.HBM((QROWS, HEAD), F32),
            pltpu.MemorySpace.HBM((QROWS, CTX), F32),
            shape((2 * SEQ, SLOT_ROWS), BF16),
            pltpu.VMEM((HELD, SLAB), BF16),
            shape((4 * SEQ, HEAD), F32),
        ),
        [SMEM] + [HBM] * 8,
        out_specs=(HBM, HBM, VMEM, VMEM, VMEM),
        scratch=[
            pltpu.SMEM((SEQ,), I32),
            pltpu.SMEM((SEQ,), I32),
            pltpu.VMEM((QROWS, HEAD), BF16),
            pltpu.VMEM((SEQ * KV, CTX, HEAD), BF16),
            pltpu.VMEM((SEQ * KV, CTX, HEAD), BF16),
            pltpu.VMEM((SEQ, SLAB), BF16),
            pltpu.VMEM((QROWS, CTX), F32),
            pltpu.VMEM((QROWS, HEAD), F32),
            pltpu.VMEM((QROWS, CTX), F32),
            *weight_scratch(1),
            pltpu.SemaphoreType.DMA((3,)),
            pltpu.SemaphoreType.DMA((6,)),
            pltpu.SemaphoreType.DMA((2,)),
        ],
        limit=24,
        cost=pl.CostEstimate(flops=1 << 30, transcendentals=1 << 16, bytes_accessed=12 << 20),
    )(
        me,
        *in_hbm(
            fill,
            adapter_choice_index,
            flat_queries,
            key_cache_rows.reshape(SEQ * KV, CTX, HEAD),
            value_cache_rows.reshape(SEQ * KV, CTX, HEAD),
            hidden,
            adapter_down_weight.reshape(ADAPTERS * RANK, SLAB),
            weight_rows,
        ),
    )
    arrived, middle, rows_here = lax.optimization_barrier((arrived, middle, rows_here))
    sums = call(
        down_kernel,
        shape((RANK, SLOT_ROWS), F32),
        [VMEM, VMEM, HBM],
        scratch=[
            pltpu.VMEM((ADAPTERS * RANK - HELD, SLAB), BF16),
            pltpu.SemaphoreType.DMA((len(PIECES),)),
        ],
    )(arrived, down, *in_hbm(adapter_down_weight.reshape(ADAPTERS * RANK, SLAB)))
    sums = sums + lax.ppermute(sums, "tp", [(i, i ^ 1) for i in range(ring)])
    across = lax.ppermute(sums, "tp", [(i, ring - 1 - i) for i in range(ring)])
    mask, inverse, up_halves, base = call(
        between_kernel,
        (
            shape((SLOT_ROWS, RANK * 128), BF16),
            shape((SEQ, 128), F32),
            pltpu.VMEM((KV, ADAPTERS * RANK, 2, HEAD), BF16),
            shape((4 * SEQ, HEAD), F32),
        ),
        [SMEM] + [VMEM] * 6 + [HBM] * 2,
        scratch=[
            *weight_scratch(1),
            pltpu.SemaphoreType.DMA((2,)),
            pltpu.SemaphoreType.DMA((KV,)),
        ],
        limit=24,
    )(
        me,
        arrived,
        hidden,
        *others,
        base,
        *in_hbm(adapter_up_weight.reshape(ADAPTERS * RANK, 2, KV * HEAD), weight_rows),
    )
    corrections = call(up_kernel, shape((SLOT_ROWS, KV * HEAD), BF16), [VMEM] * 4)(
        sums, across, mask, up_halves.reshape(KV, RANK * 128, HEAD)
    )
    returned = lax.all_to_all(
        corrections.reshape(owners, 8, KV * HEAD), "ad", 0, 0, tiled=True
    ).reshape(SLOT_ROWS, KV * HEAD)

    base, lift = call(
        base_kernel,
        (
            shape((4 * SEQ, HEAD), F32),
            shape((QROWS, 2 * SEQ), BF16),
        ),
        [SMEM, VMEM, VMEM, VMEM, VMEM, HBM],
        scratch=[*weight_scratch(2), pltpu.SemaphoreType.DMA((4,))],
        limit=24,
    )(me, *others[1:], inverse, base, *in_hbm(weight_rows))

    entries, context = call(
        final_kernel,
        (shape((SEQ, 2, KV, HEAD), BF16), shape((QROWS, HEAD), BF16)),
        [VMEM] * 8,
    )(hot, lift, returned, base, inverse, flat_queries, middle, level)
    return (
        entries,
        context.reshape(SEQ, KV * GROUP, HEAD),
    )


def solution(mesh):
    placed = (
        P("ad", "tp"),
        P("ad", "tp", None),
        P("ad", "tp", None, None),
        P("ad", "tp", None, None),
        P("ad"),
        P("ad"),
        P(None, None, "tp"),
        P("ad", None, "tp"),
        P("ad", None, None, "tp"),
    )
    return jax.shard_map(
        on_device,
        mesh=mesh,
        in_specs=placed,
        out_specs=(P("ad", None, "tp", None), P("ad", "tp", None)),
        check_vma=False,
    )
```

```python
import jax
import jax.numpy as jnp
from jax import lax
from jax.experimental import pallas as pl
from jax.experimental.pallas import tpu as pltpu
from jax.sharding import PartitionSpec as P

F32 = jnp.float32
BF16 = jnp.bfloat16
I32 = jnp.int32

MODEL_WIDTH = 8192
SEQ = 32
OWNERS = 32
ADAPTERS = 64
RANK = 16
HELD_PARTS = ((0, 256), (256, 256))
HELD = 512
PIECES = ((512, 256), (768, 256))
SLAB = 2048
HALF = SLAB // 2
DEPTH = 4 * SLAB
SLOT_ROWS = OWNERS * 8
KV = 2
GROUP = 8
HEAD = 128
CTX = 128
PAIRS = 4
QROWS = SEQ * KV * GROUP
adapter_scale = 0.5
epsilon = 1e-05
NEG = -1e30

VMEM = pl.BlockSpec(memory_space=pltpu.VMEM)
SMEM = pl.BlockSpec(memory_space=pltpu.SMEM)
HBM = pl.BlockSpec(memory_space=pltpu.MemorySpace.HBM)
NT = (((1,), (1,)), ((), ()))


def iota(shape, dim):
    return lax.broadcasted_iota(I32, shape, dim)


def ones_where(cond):
    return jnp.where(cond, 1.0, 0.0).astype(BF16)


def spread_ids(idx_ref, shape, dim):
    place = iota(shape, dim) & (SEQ - 1)
    out = jnp.zeros(shape, I32)
    for t in range(SEQ):
        out = jnp.where(place == t, idx_ref[t], out)
    return out


def call(kernel, out_shape, in_specs, scratch=(), out_specs=None, limit=16, cost=None):
    return pl.pallas_call(
        kernel,
        out_shape=out_shape,
        in_specs=in_specs,
        out_specs=out_specs if out_specs is not None else jax.tree.map(lambda _: VMEM, out_shape),
        scratch_shapes=list(scratch),
        compiler_params=pltpu.CompilerParams(vmem_limit_bytes=limit << 20),
        cost_estimate=cost,
    )


def in_hbm(*arrays):
    return [pltpu.with_memory_space_constraint(a, pltpu.MemorySpace.HBM) for a in arrays]


def slots_kernel(idx_hbm, h_hbm, out_hbm, idx_ref, h_ref, out_ref, sem, out_sem):
    rows_copy = pltpu.make_async_copy(h_hbm, h_ref, sem.at[0])
    ids_copy = pltpu.make_async_copy(idx_hbm, idx_ref, sem.at[1])
    ids_copy.start()
    rows_copy.start()
    ids_copy.wait()
    shape = (SEQ, 2 * SEQ)
    along = spread_ids(idx_ref, shape, 1)
    down = spread_ids(idx_ref, shape, 0)
    lane = iota(shape, 1)
    earlier = ((along >> 6) == (down >> 6)) & (iota(shape, 0) < (lane & (SEQ - 1)))
    place = jnp.sum(earlier.astype(I32), axis=0, keepdims=True)
    target = (along[0:1] >> 6) * 8 + place + 4 * (lane[0:1] >> 5)
    hot = ones_where(iota((SLOT_ROWS, 2 * SEQ), 0) == target)
    local = spread_ids(idx_ref, (2 * SEQ, 128), 0) & (ADAPTERS - 1)
    mark = ones_where(iota((2 * SEQ, 128), 1) == 2 * local + (iota((2 * SEQ, 128), 0) >> 5))
    out_ref[:, HALF:] = jnp.dot(hot, mark, preferred_element_type=F32).astype(BF16)
    rows_copy.wait()
    rows = jnp.concatenate([h_ref[:, :HALF], h_ref[:, HALF:]], axis=0)
    copies = []
    for n in range(4):
        part = slice(SLOT_ROWS // 4 * n, SLOT_ROWS // 4 * (n + 1))
        out_ref[part, :HALF] = jnp.dot(hot[part], rows, preferred_element_type=F32).astype(BF16)
        copies.append(pltpu.make_async_copy(out_ref.at[part], out_hbm.at[part], out_sem.at[n]))
        copies[n].start()
    for copy in copies:
        copy.wait()


def down_kernel(r_ref, held_ref, d_hbm, t_ref, d_ref, sem):
    copies = []
    for n, (start, count) in enumerate(PIECES):
        rows = pl.ds(start - HELD, count)
        copies.append(
            pltpu.make_async_copy(d_hbm.at[pl.ds(start, count)], d_ref.at[rows], sem.at[n])
        )
        copies[n].start()
    marks = r_ref[:, HALF:]
    pick = ones_where((iota((ADAPTERS, 128), 1) >> 1) == iota((ADAPTERS, 128), 0))
    chosen = lax.dot_general(pick, marks, NT, preferred_element_type=F32)
    rows = r_ref[:, :HALF]

    def product(part, start, count):
        first = ((iota((count, SLOT_ROWS), 1) >> 2) & 1) == 0
        g0 = lax.dot_general(part[:, :HALF], rows, NT, preferred_element_type=F32)
        g1 = lax.dot_general(part[:, HALF:], rows, NT, preferred_element_type=F32)
        g = jnp.where(first, g0, g1).reshape(count // RANK, RANK, SLOT_ROWS)
        mine = chosen[start // RANK : (start + count) // RANK]
        return jnp.sum(g * mine[:, None, :], axis=0)

    total = jnp.zeros((RANK, SLOT_ROWS), F32)
    for start, count in HELD_PARTS:
        total += product(held_ref.at[pl.ds(start, count)], start, count)
    for n, (start, count) in enumerate(PIECES):
        copies[n].wait()
        total += product(d_ref.at[pl.ds(start - HELD, count)], start, count)
    first = ((iota((RANK, SLOT_ROWS), 1) >> 2) & 1) == 0
    ahead = pltpu.roll(total, SLOT_ROWS - 4, 1)
    behind = pltpu.roll(total, 4, 1)
    t_ref[...] = total + jnp.where(first, ahead, behind)


def up_kernel(a_ref, b_ref, m_ref, u_ref, z_ref):
    latent = (a_ref[...] + b_ref[...]).astype(BF16).astype(F32)
    turned = jnp.transpose(latent).astype(BF16)
    repeat = ones_where(((iota((RANK, 256), 1) >> 1) & (RANK - 1)) == iota((RANK, 256), 0))
    wide = jnp.dot(turned, repeat, preferred_element_type=F32).astype(BF16)
    total = jnp.zeros((SLOT_ROWS, KV * HEAD), F32)
    for k in range(8):
        part = slice(256 * k, 256 * (k + 1))
        right = jnp.concatenate([u_ref[c, part, :] for c in range(KV)], axis=1)
        total += jnp.dot(wide * m_ref[:, part], right, preferred_element_type=F32)
    z_ref[...] = total.astype(BF16)


def returned_rows(idx_ref, hot_ref):
    shape = (2 * SEQ, SEQ)
    along = spread_ids(idx_ref, shape, 1)
    down = spread_ids(idx_ref, shape, 0)
    row = iota(shape, 0)
    earlier = ((along >> 6) == (down >> 6)) & (iota(shape, 1) < (row & (SEQ - 1)))
    place = jnp.sum(earlier.astype(I32), axis=1, keepdims=True)
    target = (down[:, 0:1] >> 6) * 8 + place + 4 * (row[:, 0:1] >> 5)
    hot_ref[...] = ones_where(iota((2 * SEQ, SLOT_ROWS), 1) == target)
def query_tokens(lift_ref):
    lift_row = iota((QROWS, 2 * SEQ), 0)
    lift_ref[...] = ones_where(
        iota((QROWS, 2 * SEQ), 1) == ((lift_row >> 3) & 1) * SEQ + (lift_row >> 4)
    )


def inverse_rms(shards):
    squares = jnp.zeros((SEQ, 128), F32)
    for shard in shards:
        for i in range(SLAB // 128):
            wide = shard[:, 128 * i : 128 * (i + 1)].astype(F32)
            squares += wide * wide
    mean = jnp.sum(squares, axis=1, keepdims=True) / MODEL_WIDTH
    return jnp.broadcast_to(lax.rsqrt(mean + epsilon), (SEQ, 128))


def start_weights(tp_ref, steps, w_ref, buf, sem):
    me = tp_ref[0]
    copies = []
    for n, s in enumerate(steps):
        for k in range(2):
            start = pl.multiple_of(((me + s) & 3) * DEPTH + k * (DEPTH // 2), DEPTH // 2)
            place = 2 * n + k
            copies.append(
                pltpu.make_async_copy(
                    w_ref.at[pl.ds(start, DEPTH // 2)], buf.at[place], sem.at[place]
                )
            )
            copies[place].start()
    return copies


def base_part(shards, inverse, copies, buf, left_ref):
    place = iota((SEQ, 512), 1) & 3
    spread = ones_where((iota((128, 512), 1) >> 2) == iota((128, 512), 0))
    total = jnp.zeros((4 * SEQ, HEAD), F32)
    for n, shard in enumerate(shards):
        blocks = [shard[:, 128 * i : 128 * (i + 1)] for i in range(SLAB // 128)]
        if inverse is not None:
            blocks = [(block.astype(F32) * inverse).astype(BF16) for block in blocks]
        wide = jnp.dot(jnp.concatenate(blocks, axis=0), spread, preferred_element_type=F32)
        for i in range(SLAB // 128):
            one = wide[SEQ * i : SEQ * (i + 1)]
            for k in range(4):
                left_ref[SEQ * k : SEQ * (k + 1), 512 * i : 512 * (i + 1)] = jnp.where(
                    place == k, one, 0.0
                ).astype(BF16)
        for k in range(2):
            copies[2 * n + k].wait()
            total += jnp.dot(
                left_ref[:, DEPTH // 2 * k : DEPTH // 2 * (k + 1)],
                buf[2 * n + k],
                preferred_element_type=F32,
            )
    return total


def attend_kernel(
    tp_ref, len_hbm, idx_hbm, q_hbm, k_hbm, v_hbm, h_hbm, d_ref, w_ref,
    mid_hbm, lse_hbm, hot_ref, d0_ref, base_ref,
    len_ref, idx_ref, q_ref, k_ref, v_ref, h_ref, s_ref, mid_ref, lse_ref, buf, left_ref,
    sem, in_sem, w_sem,
):
    inputs = [
        pltpu.make_async_copy(source, target, in_sem.at[n])
        for n, (source, target) in enumerate(
            ((len_hbm, len_ref), (idx_hbm, idx_ref), (q_hbm, q_ref), (k_hbm, k_ref), (v_hbm, v_ref), (h_hbm, h_ref))
        )
    ]
    for copy in inputs:
        copy.start()
    down_copy = pltpu.make_async_copy(d_ref.at[pl.ds(0, HELD)], d0_ref, sem.at[0])
    weights = start_weights(tp_ref, (0,), w_ref, buf, w_sem)
    down_copy.start()
    inputs[0].wait()
    inputs[1].wait()
    returned_rows(idx_ref, hot_ref)
    scale = HEAD**-0.5
    lane = iota((GROUP, CTX), 1)
    inputs[2].wait()
    inputs[3].wait()
    for g in range(SEQ * KV // PAIRS):
        rows = slice(GROUP * PAIRS * g, GROUP * PAIRS * (g + 1))
        keys = k_ref[PAIRS * g : PAIRS * (g + 1)].reshape(PAIRS * CTX, HEAD)
        s = lax.dot_general(q_ref[rows, :], keys, NT, preferred_element_type=F32) * scale
        for n in range(PAIRS):
            pair = PAIRS * g + n
            own = s[GROUP * n : GROUP * (n + 1), CTX * n : CTX * (n + 1)]
            s_ref[GROUP * pair : GROUP * (pair + 1), :] = jnp.where(
                lane < len_ref[pair // KV], own, NEG
            )
    for part in range(4):
        rows = slice(QROWS // 4 * part, QROWS // 4 * (part + 1))
        s = s_ref[rows, :]
        m = jnp.max(s, axis=1, keepdims=True)
        p = jnp.exp(s - m)
        norm = jnp.broadcast_to(jnp.sum(p, axis=1, keepdims=True), p.shape)
        lse_ref[rows, :] = m + jnp.log(norm)
        s_ref[rows, :] = p / norm
    level_copy = pltpu.make_async_copy(lse_ref, lse_hbm, sem.at[1])
    level_copy.start()
    inputs[4].wait()
    for g in range(SEQ * KV // PAIRS):
        blocks = []
        for n in range(PAIRS):
            pair = PAIRS * g + n
            p = s_ref[GROUP * pair : GROUP * (pair + 1), :]
            zero = jnp.zeros_like(p)
            blocks.append(
                jnp.concatenate([p if k == n else zero for k in range(PAIRS)], axis=1)
            )
        values = v_ref[PAIRS * g : PAIRS * (g + 1)].reshape(PAIRS * CTX, HEAD)
        mid_ref[GROUP * PAIRS * g : GROUP * PAIRS * (g + 1), :] = jnp.dot(
            jnp.concatenate(blocks, axis=0).astype(BF16), values, preferred_element_type=F32
        )
    middle_copy = pltpu.make_async_copy(mid_ref, mid_hbm, sem.at[2])
    middle_copy.start()
    inputs[5].wait()
    base_ref[...] = base_part((h_ref,), None, weights, buf, left_ref)
    for copy in (down_copy, level_copy, middle_copy):
        copy.wait()


def between_kernel(
    tp_ref, r_ref, h0_ref, h1_ref, h2_ref, h3_ref, before_ref, u_ref, w_ref,
    mask_ref, inv_ref, u2_ref, out_ref, buf, left_ref, w_sem, sem,
):
    copies = [
        pltpu.make_async_copy(u_ref.at[:, :, pl.ds(HEAD * c, HEAD)], u2_ref.at[c], sem.at[c])
        for c in range(KV)
    ]
    for copy in copies:
        copy.start()
    weights = start_weights(tp_ref, (1,), w_ref, buf, w_sem)
    q = iota((128, RANK * 128), 1)
    spread = ones_where(iota((128, RANK * 128), 0) == 2 * (q >> 5) + (q & 1))
    mask_ref[...] = jnp.dot(r_ref[:, HALF:], spread, preferred_element_type=F32).astype(BF16)
    inverse = inverse_rms((h0_ref, h1_ref, h2_ref, h3_ref))
    inv_ref[...] = inverse
    total = base_part((h1_ref,), inverse, weights, buf, left_ref)
    for k in range(4):
        rows = slice(SEQ * k, SEQ * (k + 1))
        out_ref[rows, :] = total[rows] + before_ref[rows, :] * inverse
    for copy in copies:
        copy.wait()


def base_kernel(
    tp_ref, h2_ref, h3_ref, inv_ref, before_ref, w_ref,
    out_ref, lift_ref, buf, left_ref, sem,
):
    copies = start_weights(tp_ref, (2, 3), w_ref, buf, sem)
    query_tokens(lift_ref)
    out_ref[...] = before_ref[...] + base_part(
        (h2_ref, h3_ref), inv_ref[...], copies, buf, left_ref
    )


def final_kernel(hot_ref, lift_ref, z_ref, base_ref, inv_ref, q_ref, mid_ref, lse_ref, kv_ref, ctx_ref):
    lift = lift_ref[...]
    delta = jnp.dot(hot_ref[...], z_ref[...], preferred_element_type=F32)
    inverse = inv_ref[...]
    fresh = {}
    for j in range(2):
        for c in range(KV):
            plain = base_ref[SEQ * (2 * c + j) : SEQ * (2 * c + j + 1), :]
            extra = delta[SEQ * j : SEQ * (j + 1), HEAD * c : HEAD * (c + 1)]
            fresh[j, c] = (plain + adapter_scale * inverse * extra).astype(BF16)
            kv_ref[:, j, c, :] = fresh[j, c]
    new_key = jnp.dot(lift, jnp.concatenate([fresh[0, 0], fresh[0, 1]], axis=0), preferred_element_type=F32)
    new_value = jnp.dot(lift, jnp.concatenate([fresh[1, 0], fresh[1, 1]], axis=0), preferred_element_type=F32)
    own = jnp.sum(q_ref[...].astype(F32) * new_key, axis=1, keepdims=True) * (HEAD**-0.5)
    gap = own - lse_ref[...]
    small = jnp.exp(-jnp.abs(gap))
    share = jnp.where(gap > 0, 1.0, small) / (1.0 + small)
    own_weight = share.astype(BF16).astype(F32)
    ctx_ref[...] = (mid_ref[...] * (1.0 - share) + own_weight * new_value).astype(BF16)


def on_device(
    hidden,
    queries,
    key_cache_rows,
    value_cache_rows,
    cache_fill_length,
    adapter_choice_index,
    key_value_weight,
    adapter_down_weight,
    adapter_up_weight,
):
    shape = jax.ShapeDtypeStruct
    owners = lax.axis_size("ad")
    ring = lax.axis_size("tp")

    slots = call(
        slots_kernel,
        shape((SLOT_ROWS, HALF + 128), BF16),
        [HBM, HBM],
        out_specs=HBM,
        scratch=[
            pltpu.SMEM((SEQ,), I32),
            pltpu.VMEM((SEQ, SLAB), BF16),
            pltpu.VMEM((SLOT_ROWS, HALF + 128), BF16),
            pltpu.SemaphoreType.DMA((2,)),
            pltpu.SemaphoreType.DMA((4,)),
        ],
    )(*in_hbm(adapter_choice_index, hidden))
    slots, rows_here, fill = lax.optimization_barrier((slots, hidden, cache_fill_length))
    arrived = lax.all_to_all(
        slots.reshape(owners, 8, HALF + 128), "ad", 0, 0, tiled=True
    ).reshape(SLOT_ROWS, HALF + 128)

    others = [
        lax.ppermute(rows_here, "tp", [(i, (i - s) % ring) for i in range(ring)]) for s in (1, 2, 3)
    ]
    flat_queries = queries.reshape(QROWS, HEAD)
    me = lax.axis_index("tp").astype(I32).reshape(1)
    weight_rows = (
        key_value_weight.reshape(MODEL_WIDTH, 2, KV, HEAD)
        .transpose(0, 2, 1, 3)
        .reshape(4 * MODEL_WIDTH, HEAD)
    )

    def weight_scratch(count):
        return [
            pltpu.VMEM((2 * count, DEPTH // 2, HEAD), BF16),
            pltpu.VMEM((4 * SEQ, DEPTH), BF16),
        ]

    middle, level, hot, down, base = call(
        attend_kernel,
        (
            pltpu.MemorySpace.HBM((QROWS, HEAD), F32),
            pltpu.MemorySpace.HBM((QROWS, CTX), F32),
            shape((2 * SEQ, SLOT_ROWS), BF16),
            pltpu.VMEM((HELD, SLAB), BF16),
            shape((4 * SEQ, HEAD), F32),
        ),
        [SMEM] + [HBM] * 8,
        out_specs=(HBM, HBM, VMEM, VMEM, VMEM),
        scratch=[
            pltpu.SMEM((SEQ,), I32),
            pltpu.SMEM((SEQ,), I32),
            pltpu.VMEM((QROWS, HEAD), BF16),
            pltpu.VMEM((SEQ * KV, CTX, HEAD), BF16),
            pltpu.VMEM((SEQ * KV, CTX, HEAD), BF16),
            pltpu.VMEM((SEQ, SLAB), BF16),
            pltpu.VMEM((QROWS, CTX), F32),
            pltpu.VMEM((QROWS, HEAD), F32),
            pltpu.VMEM((QROWS, CTX), F32),
            *weight_scratch(1),
            pltpu.SemaphoreType.DMA((3,)),
            pltpu.SemaphoreType.DMA((6,)),
            pltpu.SemaphoreType.DMA((2,)),
        ],
        limit=24,
        cost=pl.CostEstimate(flops=1 << 30, transcendentals=1 << 16, bytes_accessed=12 << 20),
    )(
        me,
        *in_hbm(
            fill,
            adapter_choice_index,
            flat_queries,
            key_cache_rows.reshape(SEQ * KV, CTX, HEAD),
            value_cache_rows.reshape(SEQ * KV, CTX, HEAD),
            hidden,
            adapter_down_weight.reshape(ADAPTERS * RANK, SLAB),
            weight_rows,
        ),
    )
    arrived, middle, rows_here = lax.optimization_barrier((arrived, middle, rows_here))
    sums = call(
        down_kernel,
        shape((RANK, SLOT_ROWS), F32),
        [VMEM, VMEM, HBM],
        scratch=[
            pltpu.VMEM((ADAPTERS * RANK - HELD, SLAB), BF16),
            pltpu.SemaphoreType.DMA((len(PIECES),)),
        ],
    )(arrived, down, *in_hbm(adapter_down_weight.reshape(ADAPTERS * RANK, SLAB)))
    sums = sums + lax.ppermute(sums, "tp", [(i, ring - 1 - i) for i in range(ring)])
    across = lax.ppermute(sums, "tp", [(i, i ^ 1) for i in range(ring)])
    mask, inverse, up_halves, base = call(
        between_kernel,
        (
            shape((SLOT_ROWS, RANK * 128), BF16),
            shape((SEQ, 128), F32),
            pltpu.VMEM((KV, ADAPTERS * RANK, 2, HEAD), BF16),
            shape((4 * SEQ, HEAD), F32),
        ),
        [SMEM] + [VMEM] * 6 + [HBM] * 2,
        scratch=[
            *weight_scratch(1),
            pltpu.SemaphoreType.DMA((2,)),
            pltpu.SemaphoreType.DMA((KV,)),
        ],
        limit=24,
    )(
        me,
        arrived,
        hidden,
        *others,
        base,
        *in_hbm(adapter_up_weight.reshape(ADAPTERS * RANK, 2, KV * HEAD), weight_rows),
    )
    corrections = call(up_kernel, shape((SLOT_ROWS, KV * HEAD), BF16), [VMEM] * 4)(
        sums, across, mask, up_halves.reshape(KV, RANK * 128, HEAD)
    )
    returned = lax.all_to_all(
        corrections.reshape(owners, 8, KV * HEAD), "ad", 0, 0, tiled=True
    ).reshape(SLOT_ROWS, KV * HEAD)

    base, lift = call(
        base_kernel,
        (
            shape((4 * SEQ, HEAD), F32),
            shape((QROWS, 2 * SEQ), BF16),
        ),
        [SMEM, VMEM, VMEM, VMEM, VMEM, HBM],
        scratch=[*weight_scratch(2), pltpu.SemaphoreType.DMA((4,))],
        limit=24,
    )(me, *others[1:], inverse, base, *in_hbm(weight_rows))

    entries, context = call(
        final_kernel,
        (shape((SEQ, 2, KV, HEAD), BF16), shape((QROWS, HEAD), BF16)),
        [VMEM] * 8,
    )(hot, lift, returned, base, inverse, flat_queries, middle, level)
    return (
        entries,
        context.reshape(SEQ, KV * GROUP, HEAD),
    )


def solution(mesh):
    placed = (
        P("ad", "tp"),
        P("ad", "tp", None),
        P("ad", "tp", None, None),
        P("ad", "tp", None, None),
        P("ad"),
        P("ad"),
        P(None, None, "tp"),
        P("ad", None, "tp"),
        P("ad", None, None, "tp"),
    )
    return jax.shard_map(
        on_device,
        mesh=mesh,
        in_specs=placed,
        out_specs=(P("ad", None, "tp", None), P("ad", "tp", None)),
        check_vma=False,
    )
```

```python
import jax
import jax.numpy as jnp
from jax import lax
from jax.experimental import pallas as pl
from jax.experimental.pallas import tpu as pltpu
from jax.sharding import PartitionSpec as P

F32 = jnp.float32
BF16 = jnp.bfloat16
I32 = jnp.int32

MODEL_WIDTH = 8192
SEQ = 32
OWNERS = 32
ADAPTERS = 64
RANK = 16
HELD_PARTS = ((0, 256), (256, 256), (512, 96))
HELD = 608
PIECES = ((608, 416),)
SLAB = 2048
HALF = SLAB // 2
DEPTH = 4 * SLAB
SLOT_ROWS = OWNERS * 8
KV = 2
GROUP = 8
HEAD = 128
CTX = 128
PAIRS = 4
QROWS = SEQ * KV * GROUP
adapter_scale = 0.5
epsilon = 1e-05
NEG = -1e30

VMEM = pl.BlockSpec(memory_space=pltpu.VMEM)
SMEM = pl.BlockSpec(memory_space=pltpu.SMEM)
HBM = pl.BlockSpec(memory_space=pltpu.MemorySpace.HBM)
NT = (((1,), (1,)), ((), ()))


def iota(shape, dim):
    return lax.broadcasted_iota(I32, shape, dim)


def ones_where(cond):
    return jnp.where(cond, 1.0, 0.0).astype(BF16)


def spread_ids(idx_ref, shape, dim):
    place = iota(shape, dim) & (SEQ - 1)
    out = jnp.zeros(shape, I32)
    for t in range(SEQ):
        out = jnp.where(place == t, idx_ref[t], out)
    return out


def call(kernel, out_shape, in_specs, scratch=(), out_specs=None, limit=16, cost=None):
    return pl.pallas_call(
        kernel,
        out_shape=out_shape,
        in_specs=in_specs,
        out_specs=out_specs if out_specs is not None else jax.tree.map(lambda _: VMEM, out_shape),
        scratch_shapes=list(scratch),
        compiler_params=pltpu.CompilerParams(vmem_limit_bytes=limit << 20),
        cost_estimate=cost,
    )


def in_hbm(*arrays):
    return [pltpu.with_memory_space_constraint(a, pltpu.MemorySpace.HBM) for a in arrays]


def slots_kernel(idx_hbm, h_hbm, out_hbm, idx_ref, h_ref, out_ref, sem, out_sem):
    rows_copy = pltpu.make_async_copy(h_hbm, h_ref, sem.at[0])
    ids_copy = pltpu.make_async_copy(idx_hbm, idx_ref, sem.at[1])
    ids_copy.start()
    rows_copy.start()
    ids_copy.wait()
    shape = (SEQ, 2 * SEQ)
    along = spread_ids(idx_ref, shape, 1)
    down = spread_ids(idx_ref, shape, 0)
    lane = iota(shape, 1)
    earlier = ((along >> 6) == (down >> 6)) & (iota(shape, 0) < (lane & (SEQ - 1)))
    place = jnp.sum(earlier.astype(I32), axis=0, keepdims=True)
    target = (along[0:1] >> 6) * 8 + place + 4 * (lane[0:1] >> 5)
    hot = ones_where(iota((SLOT_ROWS, 2 * SEQ), 0) == target)
    local = spread_ids(idx_ref, (2 * SEQ, 128), 0) & (ADAPTERS - 1)
    mark = ones_where(iota((2 * SEQ, 128), 1) == 2 * local + (iota((2 * SEQ, 128), 0) >> 5))
    out_ref[:, HALF:] = jnp.dot(hot, mark, preferred_element_type=F32).astype(BF16)
    rows_copy.wait()
    rows = jnp.concatenate([h_ref[:, :HALF], h_ref[:, HALF:]], axis=0)
    copies = []
    for n in range(4):
        part = slice(SLOT_ROWS // 4 * n, SLOT_ROWS // 4 * (n + 1))
        out_ref[part, :HALF] = jnp.dot(hot[part], rows, preferred_element_type=F32).astype(BF16)
        copies.append(pltpu.make_async_copy(out_ref.at[part], out_hbm.at[part], out_sem.at[n]))
        copies[n].start()
    for copy in copies:
        copy.wait()


def down_kernel(r_ref, held_ref, d_hbm, t_ref, d_ref, sem):
    copies = []
    for n, (start, count) in enumerate(PIECES):
        rows = pl.ds(start - HELD, count)
        copies.append(
            pltpu.make_async_copy(d_hbm.at[pl.ds(start, count)], d_ref.at[rows], sem.at[n])
        )
        copies[n].start()
    marks = r_ref[:, HALF:]
    pick = ones_where((iota((ADAPTERS, 128), 1) >> 1) == iota((ADAPTERS, 128), 0))
    chosen = lax.dot_general(pick, marks, NT, preferred_element_type=F32)
    rows = r_ref[:, :HALF]

    def product(part, start, count):
        first = ((iota((count, SLOT_ROWS), 1) >> 2) & 1) == 0
        g0 = lax.dot_general(part[:, :HALF], rows, NT, preferred_element_type=F32)
        g1 = lax.dot_general(part[:, HALF:], rows, NT, preferred_element_type=F32)
        g = jnp.where(first, g0, g1).reshape(count // RANK, RANK, SLOT_ROWS)
        mine = chosen[start // RANK : (start + count) // RANK]
        return jnp.sum(g * mine[:, None, :], axis=0)

    total = jnp.zeros((RANK, SLOT_ROWS), F32)
    for start, count in HELD_PARTS:
        total += product(held_ref.at[pl.ds(start, count)], start, count)
    for n, (start, count) in enumerate(PIECES):
        copies[n].wait()
        total += product(d_ref.at[pl.ds(start - HELD, count)], start, count)
    first = ((iota((RANK, SLOT_ROWS), 1) >> 2) & 1) == 0
    ahead = pltpu.roll(total, SLOT_ROWS - 4, 1)
    behind = pltpu.roll(total, 4, 1)
    t_ref[...] = total + jnp.where(first, ahead, behind)


def up_kernel(a_ref, b_ref, m_ref, u_ref, z_hbm, z_ref, sem):
    latent = (a_ref[...] + b_ref[...]).astype(BF16).astype(F32)
    turned = jnp.transpose(latent).astype(BF16)
    repeat = ones_where(((iota((RANK, 256), 1) >> 1) & (RANK - 1)) == iota((RANK, 256), 0))
    wide = jnp.dot(turned, repeat, preferred_element_type=F32).astype(BF16)
    copies = []
    for n in range(2):
        rows = slice(SLOT_ROWS // 2 * n, SLOT_ROWS // 2 * (n + 1))
        total = jnp.zeros((SLOT_ROWS // 2, KV * HEAD), F32)
        for k in range(8):
            part = slice(256 * k, 256 * (k + 1))
            right = jnp.concatenate([u_ref[c, part, :] for c in range(KV)], axis=1)
            total += jnp.dot(wide[rows] * m_ref[rows, part], right, preferred_element_type=F32)
        z_ref[rows, :] = total.astype(BF16)
        copies.append(pltpu.make_async_copy(z_ref.at[rows], z_hbm.at[rows], sem.at[n]))
        copies[n].start()
    for copy in copies:
        copy.wait()


def returned_rows(idx_ref, hot_ref):
    shape = (2 * SEQ, SEQ)
    along = spread_ids(idx_ref, shape, 1)
    down = spread_ids(idx_ref, shape, 0)
    row = iota(shape, 0)
    earlier = ((along >> 6) == (down >> 6)) & (iota(shape, 1) < (row & (SEQ - 1)))
    place = jnp.sum(earlier.astype(I32), axis=1, keepdims=True)
    target = (down[:, 0:1] >> 6) * 8 + place + 4 * (row[:, 0:1] >> 5)
    hot_ref[...] = ones_where(iota((2 * SEQ, SLOT_ROWS), 1) == target)
def query_tokens(lift_ref):
    lift_row = iota((QROWS, 2 * SEQ), 0)
    lift_ref[...] = ones_where(
        iota((QROWS, 2 * SEQ), 1) == ((lift_row >> 3) & 1) * SEQ + (lift_row >> 4)
    )


def inverse_rms(shards):
    squares = jnp.zeros((SEQ, 128), F32)
    for shard in shards:
        for i in range(SLAB // 128):
            wide = shard[:, 128 * i : 128 * (i + 1)].astype(F32)
            squares += wide * wide
    mean = jnp.sum(squares, axis=1, keepdims=True) / MODEL_WIDTH
    return jnp.broadcast_to(lax.rsqrt(mean + epsilon), (SEQ, 128))


def start_weights(tp_ref, steps, w_ref, buf, sem):
    me = tp_ref[0]
    copies = []
    for n, s in enumerate(steps):
        for k in range(2):
            start = pl.multiple_of(((me + s) & 3) * DEPTH + k * (DEPTH // 2), DEPTH // 2)
            place = 2 * n + k
            copies.append(
                pltpu.make_async_copy(
                    w_ref.at[pl.ds(start, DEPTH // 2)], buf.at[place], sem.at[place]
                )
            )
            copies[place].start()
    return copies


def base_part(shards, inverse, copies, buf, left_ref):
    place = iota((SEQ, 512), 1) & 3
    spread = ones_where((iota((128, 512), 1) >> 2) == iota((128, 512), 0))
    total = jnp.zeros((4 * SEQ, HEAD), F32)
    for n, shard in enumerate(shards):
        blocks = [shard[:, 128 * i : 128 * (i + 1)] for i in range(SLAB // 128)]
        if inverse is not None:
            blocks = [(block.astype(F32) * inverse).astype(BF16) for block in blocks]
        wide = jnp.dot(jnp.concatenate(blocks, axis=0), spread, preferred_element_type=F32)
        for i in range(SLAB // 128):
            one = wide[SEQ * i : SEQ * (i + 1)]
            for k in range(4):
                left_ref[SEQ * k : SEQ * (k + 1), 512 * i : 512 * (i + 1)] = jnp.where(
                    place == k, one, 0.0
                ).astype(BF16)
        for k in range(2):
            copies[2 * n + k].wait()
            total += jnp.dot(
                left_ref[:, DEPTH // 2 * k : DEPTH // 2 * (k + 1)],
                buf[2 * n + k],
                preferred_element_type=F32,
            )
    return total


def attend_kernel(
    tp_ref, len_hbm, idx_hbm, q_hbm, k_hbm, v_hbm, h_hbm, d_ref, w_ref,
    mid_hbm, lse_hbm, hot_hbm, d0_ref, base_ref,
    len_ref, idx_ref, q_ref, k_ref, v_ref, h_ref, s_ref, mid_ref, lse_ref, hot_ref, buf, left_ref,
    sem, in_sem, w_sem,
):
    inputs = [
        pltpu.make_async_copy(source, target, in_sem.at[n])
        for n, (source, target) in enumerate(
            ((len_hbm, len_ref), (idx_hbm, idx_ref), (q_hbm, q_ref), (k_hbm, k_ref), (v_hbm, v_ref), (h_hbm, h_ref))
        )
    ]
    for copy in inputs:
        copy.start()
    down_copy = pltpu.make_async_copy(d_ref.at[pl.ds(0, HELD)], d0_ref, sem.at[0])
    weights = start_weights(tp_ref, (0,), w_ref, buf, w_sem)
    down_copy.start()
    inputs[0].wait()
    inputs[1].wait()
    returned_rows(idx_ref, hot_ref)
    hot_copy = pltpu.make_async_copy(hot_ref, hot_hbm, sem.at[3])
    hot_copy.start()
    scale = HEAD**-0.5
    lane = iota((GROUP, CTX), 1)
    inputs[2].wait()
    inputs[3].wait()
    for g in range(SEQ * KV // PAIRS):
        rows = slice(GROUP * PAIRS * g, GROUP * PAIRS * (g + 1))
        keys = k_ref[PAIRS * g : PAIRS * (g + 1)].reshape(PAIRS * CTX, HEAD)
        s = lax.dot_general(q_ref[rows, :], keys, NT, preferred_element_type=F32) * scale
        for n in range(PAIRS):
            pair = PAIRS * g + n
            own = s[GROUP * n : GROUP * (n + 1), CTX * n : CTX * (n + 1)]
            s_ref[GROUP * pair : GROUP * (pair + 1), :] = jnp.where(
                lane < len_ref[pair // KV], own, NEG
            )
    for part in range(4):
        rows = slice(QROWS // 4 * part, QROWS // 4 * (part + 1))
        s = s_ref[rows, :]
        m = jnp.max(s, axis=1, keepdims=True)
        p = jnp.exp(s - m)
        norm = jnp.broadcast_to(jnp.sum(p, axis=1, keepdims=True), p.shape)
        lse_ref[rows, :] = m + jnp.log(norm)
        s_ref[rows, :] = p / norm
    level_copy = pltpu.make_async_copy(lse_ref, lse_hbm, sem.at[1])
    level_copy.start()
    inputs[4].wait()
    for g in range(SEQ * KV // PAIRS):
        blocks = []
        for n in range(PAIRS):
            pair = PAIRS * g + n
            p = s_ref[GROUP * pair : GROUP * (pair + 1), :]
            zero = jnp.zeros_like(p)
            blocks.append(
                jnp.concatenate([p if k == n else zero for k in range(PAIRS)], axis=1)
            )
        values = v_ref[PAIRS * g : PAIRS * (g + 1)].reshape(PAIRS * CTX, HEAD)
        mid_ref[GROUP * PAIRS * g : GROUP * PAIRS * (g + 1), :] = jnp.dot(
            jnp.concatenate(blocks, axis=0).astype(BF16), values, preferred_element_type=F32
        )
    middle_copy = pltpu.make_async_copy(mid_ref, mid_hbm, sem.at[2])
    middle_copy.start()
    inputs[5].wait()
    base_ref[...] = base_part((h_ref,), None, weights, buf, left_ref)
    for copy in (down_copy, level_copy, middle_copy, hot_copy):
        copy.wait()


def between_kernel(
    tp_ref, r_ref, h0_ref, h1_ref, h2_ref, h3_ref, before_ref, u_ref, w_ref,
    mask_ref, inv_ref, u2_ref, out_ref, buf, left_ref, w_sem, sem,
):
    copies = [
        pltpu.make_async_copy(u_ref.at[:, :, pl.ds(HEAD * c, HEAD)], u2_ref.at[c], sem.at[c])
        for c in range(KV)
    ]
    for copy in copies:
        copy.start()
    weights = start_weights(tp_ref, (1,), w_ref, buf, w_sem)
    q = iota((128, RANK * 128), 1)
    spread = ones_where(iota((128, RANK * 128), 0) == 2 * (q >> 5) + (q & 1))
    mask_ref[...] = jnp.dot(r_ref[:, HALF:], spread, preferred_element_type=F32).astype(BF16)
    inverse = inverse_rms((h0_ref, h1_ref, h2_ref, h3_ref))
    inv_ref[...] = inverse
    total = base_part((h1_ref,), inverse, weights, buf, left_ref)
    for k in range(4):
        rows = slice(SEQ * k, SEQ * (k + 1))
        out_ref[rows, :] = total[rows] + before_ref[rows, :] * inverse
    for copy in copies:
        copy.wait()


def base_kernel(
    tp_ref, h2_ref, h3_ref, inv_ref, before_ref, w_ref,
    out_ref, lift_ref, buf, left_ref, sem,
):
    copies = start_weights(tp_ref, (2, 3), w_ref, buf, sem)
    query_tokens(lift_ref)
    out_ref[...] = before_ref[...] + base_part(
        (h2_ref, h3_ref), inv_ref[...], copies, buf, left_ref
    )


def final_kernel(hot_ref, lift_ref, z_ref, base_ref, inv_ref, q_ref, mid_ref, lse_ref, kv_ref, ctx_ref):
    lift = lift_ref[...]
    delta = jnp.dot(hot_ref[...], z_ref[...], preferred_element_type=F32)
    inverse = inv_ref[...]
    fresh = {}
    for j in range(2):
        for c in range(KV):
            plain = base_ref[SEQ * (2 * c + j) : SEQ * (2 * c + j + 1), :]
            extra = delta[SEQ * j : SEQ * (j + 1), HEAD * c : HEAD * (c + 1)]
            fresh[j, c] = (plain + adapter_scale * inverse * extra).astype(BF16)
            kv_ref[:, j, c, :] = fresh[j, c]
    new_key = jnp.dot(lift, jnp.concatenate([fresh[0, 0], fresh[0, 1]], axis=0), preferred_element_type=F32)
    new_value = jnp.dot(lift, jnp.concatenate([fresh[1, 0], fresh[1, 1]], axis=0), preferred_element_type=F32)
    own = jnp.sum(q_ref[...].astype(F32) * new_key, axis=1, keepdims=True) * (HEAD**-0.5)
    gap = own - lse_ref[...]
    small = jnp.exp(-jnp.abs(gap))
    share = jnp.where(gap > 0, 1.0, small) / (1.0 + small)
    own_weight = share.astype(BF16).astype(F32)
    ctx_ref[...] = (mid_ref[...] * (1.0 - share) + own_weight * new_value).astype(BF16)


def on_device(
    hidden,
    queries,
    key_cache_rows,
    value_cache_rows,
    cache_fill_length,
    adapter_choice_index,
    key_value_weight,
    adapter_down_weight,
    adapter_up_weight,
):
    shape = jax.ShapeDtypeStruct
    owners = lax.axis_size("ad")
    ring = lax.axis_size("tp")

    slots = call(
        slots_kernel,
        shape((SLOT_ROWS, HALF + 128), BF16),
        [HBM, HBM],
        out_specs=HBM,
        scratch=[
            pltpu.SMEM((SEQ,), I32),
            pltpu.VMEM((SEQ, SLAB), BF16),
            pltpu.VMEM((SLOT_ROWS, HALF + 128), BF16),
            pltpu.SemaphoreType.DMA((2,)),
            pltpu.SemaphoreType.DMA((4,)),
        ],
    )(*in_hbm(adapter_choice_index, hidden))
    slots, rows_here, fill = lax.optimization_barrier((slots, hidden, cache_fill_length))
    arrived = lax.all_to_all(
        slots.reshape(owners, 8, HALF + 128), "ad", 0, 0, tiled=True
    ).reshape(SLOT_ROWS, HALF + 128)

    others = [
        lax.ppermute(rows_here, "tp", [(i, (i - s) % ring) for i in range(ring)]) for s in (1, 2, 3)
    ]
    flat_queries = queries.reshape(QROWS, HEAD)
    me = lax.axis_index("tp").astype(I32).reshape(1)
    weight_rows = (
        key_value_weight.reshape(MODEL_WIDTH, 2, KV, HEAD)
        .transpose(0, 2, 1, 3)
        .reshape(4 * MODEL_WIDTH, HEAD)
    )

    def weight_scratch(count):
        return [
            pltpu.VMEM((2 * count, DEPTH // 2, HEAD), BF16),
            pltpu.VMEM((4 * SEQ, DEPTH), BF16),
        ]

    middle, level, hot, down, base = call(
        attend_kernel,
        (
            pltpu.MemorySpace.HBM((QROWS, HEAD), F32),
            pltpu.MemorySpace.HBM((QROWS, CTX), F32),
            pltpu.MemorySpace.HBM((2 * SEQ, SLOT_ROWS), BF16),
            pltpu.VMEM((HELD, SLAB), BF16),
            shape((4 * SEQ, HEAD), F32),
        ),
        [SMEM] + [HBM] * 8,
        out_specs=(HBM, HBM, HBM, VMEM, VMEM),
        scratch=[
            pltpu.SMEM((SEQ,), I32),
            pltpu.SMEM((SEQ,), I32),
            pltpu.VMEM((QROWS, HEAD), BF16),
            pltpu.VMEM((SEQ * KV, CTX, HEAD), BF16),
            pltpu.VMEM((SEQ * KV, CTX, HEAD), BF16),
            pltpu.VMEM((SEQ, SLAB), BF16),
            pltpu.VMEM((QROWS, CTX), F32),
            pltpu.VMEM((QROWS, HEAD), F32),
            pltpu.VMEM((QROWS, CTX), F32),
            pltpu.VMEM((2 * SEQ, SLOT_ROWS), BF16),
            *weight_scratch(1),
            pltpu.SemaphoreType.DMA((4,)),
            pltpu.SemaphoreType.DMA((6,)),
            pltpu.SemaphoreType.DMA((2,)),
        ],
        limit=24,
        cost=pl.CostEstimate(flops=1 << 30, transcendentals=1 << 16, bytes_accessed=12 << 20),
    )(
        me,
        *in_hbm(
            fill,
            adapter_choice_index,
            flat_queries,
            key_cache_rows.reshape(SEQ * KV, CTX, HEAD),
            value_cache_rows.reshape(SEQ * KV, CTX, HEAD),
            hidden,
            adapter_down_weight.reshape(ADAPTERS * RANK, SLAB),
            weight_rows,
        ),
    )
    arrived, middle, rows_here = lax.optimization_barrier((arrived, middle, rows_here))
    sums = call(
        down_kernel,
        shape((RANK, SLOT_ROWS), F32),
        [VMEM, VMEM, HBM],
        scratch=[
            pltpu.VMEM((ADAPTERS * RANK - HELD, SLAB), BF16),
            pltpu.SemaphoreType.DMA((len(PIECES),)),
        ],
    )(arrived, down, *in_hbm(adapter_down_weight.reshape(ADAPTERS * RANK, SLAB)))
    sums = sums + lax.ppermute(sums, "tp", [(i, ring - 1 - i) for i in range(ring)])
    across = lax.ppermute(sums, "tp", [(i, i ^ 1) for i in range(ring)])
    mask, inverse, up_halves, base = call(
        between_kernel,
        (
            shape((SLOT_ROWS, RANK * 128), BF16),
            shape((SEQ, 128), F32),
            pltpu.VMEM((KV, ADAPTERS * RANK, 2, HEAD), BF16),
            shape((4 * SEQ, HEAD), F32),
        ),
        [SMEM] + [VMEM] * 6 + [HBM] * 2,
        scratch=[
            *weight_scratch(1),
            pltpu.SemaphoreType.DMA((2,)),
            pltpu.SemaphoreType.DMA((KV,)),
        ],
        limit=24,
    )(
        me,
        arrived,
        hidden,
        *others,
        base,
        *in_hbm(adapter_up_weight.reshape(ADAPTERS * RANK, 2, KV * HEAD), weight_rows),
    )
    corrections = call(
        up_kernel,
        shape((SLOT_ROWS, KV * HEAD), BF16),
        [VMEM] * 4,
        out_specs=HBM,
        scratch=[pltpu.VMEM((SLOT_ROWS, KV * HEAD), BF16), pltpu.SemaphoreType.DMA((2,))],
    )(
        sums, across, mask, up_halves.reshape(KV, RANK * 128, HEAD)
    )
    returned = lax.all_to_all(
        corrections.reshape(owners, 8, KV * HEAD), "ad", 0, 0, tiled=True
    ).reshape(SLOT_ROWS, KV * HEAD)

    base, lift = call(
        base_kernel,
        (
            shape((4 * SEQ, HEAD), F32),
            shape((QROWS, 2 * SEQ), BF16),
        ),
        [SMEM, VMEM, VMEM, VMEM, VMEM, HBM],
        scratch=[*weight_scratch(2), pltpu.SemaphoreType.DMA((4,))],
        limit=24,
    )(me, *others[1:], inverse, base, *in_hbm(weight_rows))

    entries, context = call(
        final_kernel,
        (shape((SEQ, 2, KV, HEAD), BF16), shape((QROWS, HEAD), BF16)),
        [VMEM] * 8,
    )(hot, lift, returned, base, inverse, flat_queries, middle, level)
    return (
        entries,
        context.reshape(SEQ, KV * GROUP, HEAD),
    )


def solution(mesh):
    placed = (
        P("ad", "tp"),
        P("ad", "tp", None),
        P("ad", "tp", None, None),
        P("ad", "tp", None, None),
        P("ad"),
        P("ad"),
        P(None, None, "tp"),
        P("ad", None, "tp"),
        P("ad", None, None, "tp"),
    )
    return jax.shard_map(
        on_device,
        mesh=mesh,
        in_specs=placed,
        out_specs=(P("ad", None, "tp", None), P("ad", "tp", None)),
        check_vma=False,
    )
```

```python
import jax
import jax.numpy as jnp
from jax import lax
from jax.experimental import pallas as pl
from jax.experimental.pallas import tpu as pltpu
from jax.sharding import PartitionSpec as P

F32 = jnp.float32
BF16 = jnp.bfloat16
I32 = jnp.int32

MODEL_WIDTH = 8192
SEQ = 32
OWNERS = 32
ADAPTERS = 64
RANK = 16
HELD_PARTS = ((0, 256), (256, 256))
HELD = 512
PIECES = ((512, 256), (768, 256))
SLAB = 2048
HALF = SLAB // 2
DEPTH = 4 * SLAB
SLOT_ROWS = OWNERS * 8
KV = 2
GROUP = 8
HEAD = 128
CTX = 128
PAIRS = 4
QROWS = SEQ * KV * GROUP
adapter_scale = 0.5
epsilon = 1e-05
NEG = -1e30

VMEM = pl.BlockSpec(memory_space=pltpu.VMEM)
SMEM = pl.BlockSpec(memory_space=pltpu.SMEM)
HBM = pl.BlockSpec(memory_space=pltpu.MemorySpace.HBM)
NT = (((1,), (1,)), ((), ()))


def iota(shape, dim):
    return lax.broadcasted_iota(I32, shape, dim)


def ones_where(cond):
    return jnp.where(cond, 1.0, 0.0).astype(BF16)


def spread_ids(idx_ref, shape, dim):
    place = iota(shape, dim) & (SEQ - 1)
    out = jnp.zeros(shape, I32)
    for t in range(SEQ):
        out = jnp.where(place == t, idx_ref[t], out)
    return out


def call(kernel, out_shape, in_specs, scratch=(), out_specs=None, limit=16, cost=None):
    return pl.pallas_call(
        kernel,
        out_shape=out_shape,
        in_specs=in_specs,
        out_specs=out_specs if out_specs is not None else jax.tree.map(lambda _: VMEM, out_shape),
        scratch_shapes=list(scratch),
        compiler_params=pltpu.CompilerParams(vmem_limit_bytes=limit << 20),
        cost_estimate=cost,
    )


def in_hbm(*arrays):
    return [pltpu.with_memory_space_constraint(a, pltpu.MemorySpace.HBM) for a in arrays]


def slots_kernel(idx_hbm, h_hbm, out_hbm, idx_ref, h_ref, out_ref, sem, out_sem):
    rows_copy = pltpu.make_async_copy(h_hbm, h_ref, sem.at[0])
    ids_copy = pltpu.make_async_copy(idx_hbm, idx_ref, sem.at[1])
    ids_copy.start()
    rows_copy.start()
    ids_copy.wait()
    shape = (SEQ, 2 * SEQ)
    along = spread_ids(idx_ref, shape, 1)
    down = spread_ids(idx_ref, shape, 0)
    lane = iota(shape, 1)
    earlier = ((along >> 6) == (down >> 6)) & (iota(shape, 0) < (lane & (SEQ - 1)))
    place = jnp.sum(earlier.astype(I32), axis=0, keepdims=True)
    target = (along[0:1] >> 6) * 8 + place + 4 * (lane[0:1] >> 5)
    hot = ones_where(iota((SLOT_ROWS, 2 * SEQ), 0) == target)
    local = spread_ids(idx_ref, (2 * SEQ, 128), 0) & (ADAPTERS - 1)
    mark = ones_where(iota((2 * SEQ, 128), 1) == 2 * local + (iota((2 * SEQ, 128), 0) >> 5))
    out_ref[:, HALF:] = jnp.dot(hot, mark, preferred_element_type=F32).astype(BF16)
    rows_copy.wait()
    rows = jnp.concatenate([h_ref[:, :HALF], h_ref[:, HALF:]], axis=0)
    copies = []
    for n in range(4):
        part = slice(SLOT_ROWS // 4 * n, SLOT_ROWS // 4 * (n + 1))
        out_ref[part, :HALF] = jnp.dot(hot[part], rows, preferred_element_type=F32).astype(BF16)
        copies.append(pltpu.make_async_copy(out_ref.at[part], out_hbm.at[part], out_sem.at[n]))
        copies[n].start()
    for copy in copies:
        copy.wait()


def down_kernel(r_ref, held_ref, d_hbm, t_ref, d_ref, sem):
    copies = []
    for n, (start, count) in enumerate(PIECES):
        rows = pl.ds(start - HELD, count)
        copies.append(
            pltpu.make_async_copy(d_hbm.at[pl.ds(start, count)], d_ref.at[rows], sem.at[n])
        )
        copies[n].start()
    marks = r_ref[:, HALF:]
    pick = ones_where((iota((ADAPTERS, 128), 1) >> 1) == iota((ADAPTERS, 128), 0))
    chosen = lax.dot_general(pick, marks, NT, preferred_element_type=F32)
    rows = r_ref[:, :HALF]

    def product(part, start, count):
        first = ((iota((count, SLOT_ROWS), 1) >> 2) & 1) == 0
        g0 = lax.dot_general(part[:, :HALF], rows, NT, preferred_element_type=F32)
        g1 = lax.dot_general(part[:, HALF:], rows, NT, preferred_element_type=F32)
        g = jnp.where(first, g0, g1).reshape(count // RANK, RANK, SLOT_ROWS)
        mine = chosen[start // RANK : (start + count) // RANK]
        return jnp.sum(g * mine[:, None, :], axis=0)

    total = jnp.zeros((RANK, SLOT_ROWS), F32)
    for start, count in HELD_PARTS:
        total += product(held_ref.at[pl.ds(start, count)], start, count)
    for n, (start, count) in enumerate(PIECES):
        copies[n].wait()
        total += product(d_ref.at[pl.ds(start - HELD, count)], start, count)
    first = ((iota((RANK, SLOT_ROWS), 1) >> 2) & 1) == 0
    ahead = pltpu.roll(total, SLOT_ROWS - 4, 1)
    behind = pltpu.roll(total, 4, 1)
    t_ref[...] = total + jnp.where(first, ahead, behind)


def up_kernel(a_ref, b_ref, m_ref, u_ref, z_ref):
    latent = (a_ref[...] + b_ref[...]).astype(BF16).astype(F32)
    turned = jnp.transpose(latent).astype(BF16)
    repeat = ones_where(((iota((RANK, 256), 1) >> 1) & (RANK - 1)) == iota((RANK, 256), 0))
    wide = jnp.dot(turned, repeat, preferred_element_type=F32).astype(BF16)
    total = jnp.zeros((SLOT_ROWS, KV * HEAD), F32)
    for k in range(8):
        part = slice(256 * k, 256 * (k + 1))
        right = jnp.concatenate([u_ref[c, part, :] for c in range(KV)], axis=1)
        total += jnp.dot(wide * m_ref[:, part], right, preferred_element_type=F32)
    z_ref[...] = total.astype(BF16)


def returned_rows(idx_ref, hot_ref):
    shape = (2 * SEQ, SEQ)
    along = spread_ids(idx_ref, shape, 1)
    down = spread_ids(idx_ref, shape, 0)
    row = iota(shape, 0)
    earlier = ((along >> 6) == (down >> 6)) & (iota(shape, 1) < (row & (SEQ - 1)))
    place = jnp.sum(earlier.astype(I32), axis=1, keepdims=True)
    target = (down[:, 0:1] >> 6) * 8 + place + 4 * (row[:, 0:1] >> 5)
    hot_ref[...] = ones_where(iota((2 * SEQ, SLOT_ROWS), 1) == target)
def query_tokens(lift_ref):
    lift_row = iota((QROWS, 2 * SEQ), 0)
    lift_ref[...] = ones_where(
        iota((QROWS, 2 * SEQ), 1) == ((lift_row >> 3) & 1) * SEQ + (lift_row >> 4)
    )


def inverse_rms(shards):
    squares = jnp.zeros((SEQ, 128), F32)
    for shard in shards:
        for i in range(SLAB // 128):
            wide = shard[:, 128 * i : 128 * (i + 1)].astype(F32)
            squares += wide * wide
    mean = jnp.sum(squares, axis=1, keepdims=True) / MODEL_WIDTH
    return jnp.broadcast_to(lax.rsqrt(mean + epsilon), (SEQ, 128))


def start_weights(tp_ref, steps, w_ref, buf, sem):
    me = tp_ref[0]
    copies = []
    for n, s in enumerate(steps):
        for k in range(2):
            start = pl.multiple_of(((me + s) & 3) * DEPTH + k * (DEPTH // 2), DEPTH // 2)
            place = 2 * n + k
            copies.append(
                pltpu.make_async_copy(
                    w_ref.at[pl.ds(start, DEPTH // 2)], buf.at[place], sem.at[place]
                )
            )
            copies[place].start()
    return copies


def base_part(shards, inverse, copies, buf, left_ref):
    place = iota((SEQ, 512), 1) & 3
    spread = ones_where((iota((128, 512), 1) >> 2) == iota((128, 512), 0))
    total = jnp.zeros((4 * SEQ, HEAD), F32)
    for n, shard in enumerate(shards):
        blocks = [shard[:, 128 * i : 128 * (i + 1)] for i in range(SLAB // 128)]
        if inverse is not None:
            blocks = [(block.astype(F32) * inverse).astype(BF16) for block in blocks]
        wide = jnp.dot(jnp.concatenate(blocks, axis=0), spread, preferred_element_type=F32)
        for i in range(SLAB // 128):
            one = wide[SEQ * i : SEQ * (i + 1)]
            for k in range(4):
                left_ref[SEQ * k : SEQ * (k + 1), 512 * i : 512 * (i + 1)] = jnp.where(
                    place == k, one, 0.0
                ).astype(BF16)
        for k in range(2):
            copies[2 * n + k].wait()
            total += jnp.dot(
                left_ref[:, DEPTH // 2 * k : DEPTH // 2 * (k + 1)],
                buf[2 * n + k],
                preferred_element_type=F32,
            )
    return total


def attend_kernel(
    tp_ref, len_hbm, idx_hbm, q_hbm, k_hbm, v_hbm, h_hbm, d_ref, w_ref,
    mid_hbm, lse_hbm, hot_ref, d0_ref, base_ref,
    len_ref, idx_ref, q_ref, k_ref, v_ref, h_ref, s_ref, mid_ref, lse_ref, buf, left_ref,
    sem, in_sem, w_sem,
):
    inputs = [
        pltpu.make_async_copy(source, target, in_sem.at[n])
        for n, (source, target) in enumerate(
            ((len_hbm, len_ref), (idx_hbm, idx_ref), (q_hbm, q_ref), (k_hbm, k_ref), (v_hbm, v_ref), (h_hbm, h_ref))
        )
    ]
    for copy in inputs:
        copy.start()
    down_copy = pltpu.make_async_copy(d_ref.at[pl.ds(0, HELD)], d0_ref, sem.at[0])
    weights = start_weights(tp_ref, (0,), w_ref, buf, w_sem)
    down_copy.start()
    inputs[0].wait()
    inputs[1].wait()
    returned_rows(idx_ref, hot_ref)
    scale = HEAD**-0.5
    lane = iota((GROUP, CTX), 1)
    inputs[2].wait()
    inputs[3].wait()
    for g in range(SEQ * KV // PAIRS):
        rows = slice(GROUP * PAIRS * g, GROUP * PAIRS * (g + 1))
        keys = k_ref[PAIRS * g : PAIRS * (g + 1)].reshape(PAIRS * CTX, HEAD)
        s = lax.dot_general(q_ref[rows, :], keys, NT, preferred_element_type=F32) * scale
        for n in range(PAIRS):
            pair = PAIRS * g + n
            own = s[GROUP * n : GROUP * (n + 1), CTX * n : CTX * (n + 1)]
            s_ref[GROUP * pair : GROUP * (pair + 1), :] = jnp.where(
                lane < len_ref[pair // KV], own, NEG
            )
    for part in range(4):
        rows = slice(QROWS // 4 * part, QROWS // 4 * (part + 1))
        s = s_ref[rows, :]
        m = jnp.max(s, axis=1, keepdims=True)
        p = jnp.exp(s - m)
        norm = jnp.broadcast_to(jnp.sum(p, axis=1, keepdims=True), p.shape)
        lse_ref[rows, :] = m + jnp.log(norm)
        s_ref[rows, :] = p / norm
    level_copy = pltpu.make_async_copy(lse_ref, lse_hbm, sem.at[1])
    level_copy.start()
    inputs[4].wait()
    for g in range(SEQ * KV // PAIRS):
        blocks = []
        for n in range(PAIRS):
            pair = PAIRS * g + n
            p = s_ref[GROUP * pair : GROUP * (pair + 1), :]
            zero = jnp.zeros_like(p)
            blocks.append(
                jnp.concatenate([p if k == n else zero for k in range(PAIRS)], axis=1)
            )
        values = v_ref[PAIRS * g : PAIRS * (g + 1)].reshape(PAIRS * CTX, HEAD)
        mid_ref[GROUP * PAIRS * g : GROUP * PAIRS * (g + 1), :] = jnp.dot(
            jnp.concatenate(blocks, axis=0).astype(BF16), values, preferred_element_type=F32
        )
    middle_copy = pltpu.make_async_copy(mid_ref, mid_hbm, sem.at[2])
    middle_copy.start()
    inputs[5].wait()
    base_ref[...] = base_part((h_ref,), None, weights, buf, left_ref)
    for copy in (down_copy, level_copy, middle_copy):
        copy.wait()


def mask_kernel(r_ref, u_ref, mask_ref, u2_ref, sem):
    copies = [
        pltpu.make_async_copy(u_ref.at[:, :, pl.ds(HEAD * c, HEAD)], u2_ref.at[c], sem.at[c])
        for c in range(KV)
    ]
    for copy in copies:
        copy.start()
    q = iota((128, RANK * 128), 1)
    spread = ones_where(iota((128, RANK * 128), 0) == 2 * (q >> 5) + (q & 1))
    mask_ref[...] = jnp.dot(r_ref[:, HALF:], spread, preferred_element_type=F32).astype(BF16)
    for copy in copies:
        copy.wait()


def base_second_kernel(
    tp_ref, h0_ref, h1_ref, h2_ref, h3_ref, before_ref, w_ref,
    inv_ref, out_ref, buf, left_ref, sem,
):
    weights = start_weights(tp_ref, (1,), w_ref, buf, sem)
    inverse = inverse_rms((h0_ref, h1_ref, h2_ref, h3_ref))
    inv_ref[...] = inverse
    total = base_part((h1_ref,), inverse, weights, buf, left_ref)
    for k in range(4):
        rows = slice(SEQ * k, SEQ * (k + 1))
        out_ref[rows, :] = total[rows] + before_ref[rows, :] * inverse


def base_kernel(
    tp_ref, h2_ref, h3_ref, inv_ref, before_ref, w_ref,
    out_ref, lift_ref, buf, left_ref, sem,
):
    copies = start_weights(tp_ref, (2, 3), w_ref, buf, sem)
    query_tokens(lift_ref)
    out_ref[...] = before_ref[...] + base_part(
        (h2_ref, h3_ref), inv_ref[...], copies, buf, left_ref
    )


def final_kernel(hot_ref, lift_ref, z_ref, base_ref, inv_ref, q_ref, mid_ref, lse_ref, kv_ref, ctx_ref):
    lift = lift_ref[...]
    delta = jnp.dot(hot_ref[...], z_ref[...], preferred_element_type=F32)
    inverse = inv_ref[...]
    fresh = {}
    for j in range(2):
        for c in range(KV):
            plain = base_ref[SEQ * (2 * c + j) : SEQ * (2 * c + j + 1), :]
            extra = delta[SEQ * j : SEQ * (j + 1), HEAD * c : HEAD * (c + 1)]
            fresh[j, c] = (plain + adapter_scale * inverse * extra).astype(BF16)
            kv_ref[:, j, c, :] = fresh[j, c]
    new_key = jnp.dot(lift, jnp.concatenate([fresh[0, 0], fresh[0, 1]], axis=0), preferred_element_type=F32)
    new_value = jnp.dot(lift, jnp.concatenate([fresh[1, 0], fresh[1, 1]], axis=0), preferred_element_type=F32)
    own = jnp.sum(q_ref[...].astype(F32) * new_key, axis=1, keepdims=True) * (HEAD**-0.5)
    gap = own - lse_ref[...]
    small = jnp.exp(-jnp.abs(gap))
    share = jnp.where(gap > 0, 1.0, small) / (1.0 + small)
    own_weight = share.astype(BF16).astype(F32)
    ctx_ref[...] = (mid_ref[...] * (1.0 - share) + own_weight * new_value).astype(BF16)


def on_device(
    hidden,
    queries,
    key_cache_rows,
    value_cache_rows,
    cache_fill_length,
    adapter_choice_index,
    key_value_weight,
    adapter_down_weight,
    adapter_up_weight,
):
    shape = jax.ShapeDtypeStruct
    owners = lax.axis_size("ad")
    ring = lax.axis_size("tp")

    slots = call(
        slots_kernel,
        shape((SLOT_ROWS, HALF + 128), BF16),
        [HBM, HBM],
        out_specs=HBM,
        scratch=[
            pltpu.SMEM((SEQ,), I32),
            pltpu.VMEM((SEQ, SLAB), BF16),
            pltpu.VMEM((SLOT_ROWS, HALF + 128), BF16),
            pltpu.SemaphoreType.DMA((2,)),
            pltpu.SemaphoreType.DMA((4,)),
        ],
    )(*in_hbm(adapter_choice_index, hidden))
    slots, rows_here, fill = lax.optimization_barrier((slots, hidden, cache_fill_length))
    arrived = lax.all_to_all(
        slots.reshape(owners, 8, HALF + 128), "ad", 0, 0, tiled=True
    ).reshape(SLOT_ROWS, HALF + 128)

    others = [
        lax.ppermute(rows_here, "tp", [(i, (i - s) % ring) for i in range(ring)]) for s in (1, 2, 3)
    ]
    flat_queries = queries.reshape(QROWS, HEAD)
    me = lax.axis_index("tp").astype(I32).reshape(1)
    weight_rows = (
        key_value_weight.reshape(MODEL_WIDTH, 2, KV, HEAD)
        .transpose(0, 2, 1, 3)
        .reshape(4 * MODEL_WIDTH, HEAD)
    )

    def weight_scratch(count):
        return [
            pltpu.VMEM((2 * count, DEPTH // 2, HEAD), BF16),
            pltpu.VMEM((4 * SEQ, DEPTH), BF16),
        ]

    middle, level, hot, down, base = call(
        attend_kernel,
        (
            pltpu.MemorySpace.HBM((QROWS, HEAD), F32),
            pltpu.MemorySpace.HBM((QROWS, CTX), F32),
            shape((2 * SEQ, SLOT_ROWS), BF16),
            pltpu.VMEM((HELD, SLAB), BF16),
            shape((4 * SEQ, HEAD), F32),
        ),
        [SMEM] + [HBM] * 8,
        out_specs=(HBM, HBM, VMEM, VMEM, VMEM),
        scratch=[
            pltpu.SMEM((SEQ,), I32),
            pltpu.SMEM((SEQ,), I32),
            pltpu.VMEM((QROWS, HEAD), BF16),
            pltpu.VMEM((SEQ * KV, CTX, HEAD), BF16),
            pltpu.VMEM((SEQ * KV, CTX, HEAD), BF16),
            pltpu.VMEM((SEQ, SLAB), BF16),
            pltpu.VMEM((QROWS, CTX), F32),
            pltpu.VMEM((QROWS, HEAD), F32),
            pltpu.VMEM((QROWS, CTX), F32),
            *weight_scratch(1),
            pltpu.SemaphoreType.DMA((3,)),
            pltpu.SemaphoreType.DMA((6,)),
            pltpu.SemaphoreType.DMA((2,)),
        ],
        limit=24,
        cost=pl.CostEstimate(flops=1 << 30, transcendentals=1 << 16, bytes_accessed=12 << 20),
    )(
        me,
        *in_hbm(
            fill,
            adapter_choice_index,
            flat_queries,
            key_cache_rows.reshape(SEQ * KV, CTX, HEAD),
            value_cache_rows.reshape(SEQ * KV, CTX, HEAD),
            hidden,
            adapter_down_weight.reshape(ADAPTERS * RANK, SLAB),
            weight_rows,
        ),
    )
    arrived, middle, rows_here = lax.optimization_barrier((arrived, middle, rows_here))
    sums = call(
        down_kernel,
        shape((RANK, SLOT_ROWS), F32),
        [VMEM, VMEM, HBM],
        scratch=[
            pltpu.VMEM((ADAPTERS * RANK - HELD, SLAB), BF16),
            pltpu.SemaphoreType.DMA((len(PIECES),)),
        ],
    )(arrived, down, *in_hbm(adapter_down_weight.reshape(ADAPTERS * RANK, SLAB)))
    partner = lax.ppermute(sums, "tp", [(i, ring - 1 - i) for i in range(ring)])
    rows_in, kept = lax.optimization_barrier((arrived, sums))
    mask, up_halves = call(
        mask_kernel,
        (
            shape((SLOT_ROWS, RANK * 128), BF16),
            pltpu.VMEM((KV, ADAPTERS * RANK, 2, HEAD), BF16),
        ),
        [VMEM, HBM],
        scratch=[pltpu.SemaphoreType.DMA((KV,))],
    )(rows_in, *in_hbm(adapter_up_weight.reshape(ADAPTERS * RANK, 2, KV * HEAD)))
    partner, mask = lax.optimization_barrier((partner, mask))
    sums = kept + partner
    across = lax.ppermute(sums, "tp", [(i, i ^ 1) for i in range(ring)])
    sums, base = lax.optimization_barrier((sums, base))
    inverse, base = call(
        base_second_kernel,
        (shape((SEQ, 128), F32), shape((4 * SEQ, HEAD), F32)),
        [SMEM] + [VMEM] * 5 + [HBM],
        scratch=[*weight_scratch(1), pltpu.SemaphoreType.DMA((2,))],
        limit=24,
    )(me, hidden, *others, base, *in_hbm(weight_rows))
    across, base = lax.optimization_barrier((across, base))
    corrections = call(up_kernel, shape((SLOT_ROWS, KV * HEAD), BF16), [VMEM] * 4)(
        sums, across, mask, up_halves.reshape(KV, RANK * 128, HEAD)
    )
    returned = lax.all_to_all(
        corrections.reshape(owners, 8, KV * HEAD), "ad", 0, 0, tiled=True
    ).reshape(SLOT_ROWS, KV * HEAD)

    base, lift = call(
        base_kernel,
        (
            shape((4 * SEQ, HEAD), F32),
            shape((QROWS, 2 * SEQ), BF16),
        ),
        [SMEM, VMEM, VMEM, VMEM, VMEM, HBM],
        scratch=[*weight_scratch(2), pltpu.SemaphoreType.DMA((4,))],
        limit=24,
    )(me, *others[1:], inverse, base, *in_hbm(weight_rows))

    entries, context = call(
        final_kernel,
        (shape((SEQ, 2, KV, HEAD), BF16), shape((QROWS, HEAD), BF16)),
        [VMEM] * 8,
    )(hot, lift, returned, base, inverse, flat_queries, middle, level)
    return (
        entries,
        context.reshape(SEQ, KV * GROUP, HEAD),
    )


def solution(mesh):
    placed = (
        P("ad", "tp"),
        P("ad", "tp", None),
        P("ad", "tp", None, None),
        P("ad", "tp", None, None),
        P("ad"),
        P("ad"),
        P(None, None, "tp"),
        P("ad", None, "tp"),
        P("ad", None, None, "tp"),
    )
    return jax.shard_map(
        on_device,
        mesh=mesh,
        in_specs=placed,
        out_specs=(P("ad", None, "tp", None), P("ad", "tp", None)),
        check_vma=False,
    )
```
